256 devices in a mesh: expert: 8 (over y, core), hidden: 32 (over z, x).
Axes of the slice: x: 4, y: 4, z: 8, core: 2. Of those that a mesh axis runs over, the one named last changes fastest.
Arguments:
- tokens: bfloat16 [2048, 3584], P('hidden'), may hold values from -6 to 6
- cotangent: bfloat16 [2048, 3584], P('hidden'), may hold values from -6 to 6
- routes: int32 [2048, 8], P('hidden'), may hold values from 0 to 63, all different within a row; in each aligned block of 64 rows (0 to 63, 64 to 127, ...) at most 20 rows name the same one
- route_weights: float32 [2048, 8], P('hidden'), may hold values from 0.08 to 1
- gate_weight: bfloat16 [65536, 3584], P(('expert', 'hidden')), may hold values from -0.09375 to 0.09375
- up_weight: bfloat16 [65536, 3584], P(('expert', 'hidden')), may hold values from -0.09375 to 0.09375
- down_weight: bfloat16 [65536, 3584], P(('expert', 'hidden')), may hold values from -6 to 6
- cluster: int32 [64], replicated, may hold values from 0 to 23, as said below
- merged_slot: int32 [24], replicated, may hold values from 0 to 23, each once
Outputs:
- merged_down: bfloat16 [24, 4, 256, 3584], P('expert', None, 'hidden')
The draws below stay inside these ranges and needn't reach their ends.
Inputs may be any that keep to these rules, and one draw needn't show every extreme that they name: `routes`: each row names 8 different experts. Within the rows of one shard of 64 tokens no expert is named by more than 20 rows, a bound that some block reaches. Every one of the 24 clusters has 1 to 6 member experts, and some cluster has exactly 6. `merged_slot`: each slot holds exactly one cluster.
All inputs are finite; a program needn't handle non-finite values.
Results may differ from the reference program's by a relative error of at most 0.014.
Values may be sent and summed in bfloat16 or wider, within the bound.
No kernel may reach another device: no remote copies, remote signals or barrier semaphores. Data moves between devices by JAX's collectives and lax.ppermute only.
A program may use at most 128 MiB of HBM per device.

```python
import math
import jax
import jax.numpy as jnp
import numpy as np
from jax import lax

D = 3584
F = 1024
EXPERTS = 64
MERGED = 24
TOP = 8
TOK_DEV = 64
TOKENS = 2048
CAP = 20
SLICE_ROWS = 256
SLICE_COUNT = 4
N_EXPERT = 8
N_HIDDEN = 32


def draw_cluster(key, part):
    key_big, key_grow, key_order = jax.random.split(jax.random.fold_in(key, 11), 3)
    labels = jnp.arange(MERGED, dtype=jnp.int32)
    biggest = jax.random.randint(key_big, (), 0, MERGED, dtype=jnp.int32)
    counts = jnp.ones((MERGED,), jnp.int32) + 5 * (labels == biggest).astype(jnp.int32)
    grow_keys = jax.random.split(key_grow, EXPERTS - MERGED - 5)

    def grow(counts, subkey):
        scores = jax.random.randint(subkey, (MERGED,), 0, 1 << 20, dtype=jnp.int32) * MERGED + labels
        scores = jnp.where(counts < 6, scores, -1)
        chosen = jnp.argmax(scores).astype(jnp.int32)
        return (counts + (labels == chosen).astype(jnp.int32), None)
    counts, _ = lax.scan(grow, counts, grow_keys)
    bounds = jnp.cumsum(counts)
    positions = jnp.arange(EXPERTS, dtype=jnp.int32)
    cluster_at = jnp.sum((positions[:, None] >= bounds[None, :]).astype(jnp.int32), axis=1)
    shuffle = jax.random.permutation(key_order, EXPERTS).astype(jnp.int32)
    inverse = jnp.argsort(shuffle, stable=True)
    return cluster_at[inverse].astype(jnp.int32)


def token_scales(key):
    lowest = math.log(0.1)
    highest = math.log(0.8)
    return jnp.exp(jax.random.uniform(jax.random.fold_in(key, 21), (TOKENS,), jnp.float32, lowest, highest))


def draw_route_weights(key, part):
    scales = token_scales(key)
    spread_key = jax.random.fold_in(key, 22)
    spread_part = jnp.exp(jax.random.uniform(spread_key, (TOKENS, TOP), jnp.float32, math.log(0.8), math.log(1.25)))
    return (scales[:, None] * spread_part).astype(jnp.float32)


def draw_cotangent(key, part):
    scales = token_scales(key)
    blocks = 16
    hot_block = jax.random.randint(jax.random.fold_in(key, 23), (TOKENS,), 0, blocks, dtype=jnp.int32)
    cold_gain = jnp.exp(jax.random.uniform(jax.random.fold_in(key, 24), (TOKENS, blocks), jnp.float32, -2.5, -0.5))
    block_ids = jnp.arange(blocks, dtype=jnp.int32)
    base_key = jax.random.fold_in(key, 25)
    hot_gain = 2.5
    base_values = jax.random.normal(base_key, (TOKENS, D), jnp.float32)
    block_gain = jnp.where(block_ids[None, :] == hot_block[:, None], hot_gain, cold_gain)
    column_gain = jnp.repeat(block_gain, D // blocks, axis=1)
    values = base_values * column_gain * (0.2 / scales)[:, None]
    return jnp.clip(values, -6.0, 6.0).astype(jnp.bfloat16)


def block_levels(stream_key, extent, cuts, smallest, top_value):
    loudness, own = 1.0, jax.random.fold_in(stream_key, 6)
    for axis_at, parts in cuts:
        heights = jnp.exp(jax.random.uniform(jax.random.fold_in(own, axis_at), (parts,), jnp.float32, smallest / len(cuts), top_value / len(cuts)))
        loudness = loudness * jnp.repeat(heights, extent[axis_at] // parts).reshape([-1 if axis == axis_at else 1 for axis in range(len(extent))])
    return loudness


def shared_out(rng, own, number, rows, amount, top, bound, skew):
    ranking = jax.random.permutation(rng, amount)
    crowded, common = load_shares(amount, rows * top, bound, skew, True), load_shares(amount, rows * top, bound, skew, False)
    places = jnp.arange(amount)

    def named(lengths, turn):
        used = int((lengths > 0).sum())
        fixed = max(1, used // 4)
        moved = fixed + (places - fixed + turn * (used - fixed)) % max(1, amount - fixed)
        return jnp.zeros((amount,), jnp.int32).at[ranking[jnp.where(places < fixed, places, moved)]].set(jnp.asarray(lengths, jnp.int32))

    lengths = jnp.where(number % 4 == 0, named(crowded, number // 4), named(common, number - number // 4 - 1))
    mixed = jax.random.permutation(jax.random.fold_in(own, 3), amount)
    giver, taker = mixed[0:amount // 2 * 2:2], mixed[1:amount // 2 * 2:2]
    margin = jnp.minimum(lengths[giver] - 1, bound - lengths[taker]) // 2
    margin = jnp.where((giver == ranking[0]) | (taker == ranking[0]) | (lengths[taker] == 0), 0, jnp.maximum(margin, 0))
    moved = jax.random.randint(jax.random.fold_in(own, 4), (amount // 2,), 0, 1 << 20) % (margin + 1)
    lengths = lengths.at[giver].add(-moved).at[taker].add(moved)
    items = jnp.searchsorted(jnp.cumsum(lengths), jnp.arange(rows * top), side="right").astype(jnp.int32)
    grid = items.reshape(top, rows).T
    grid = grid[jax.random.permutation(jax.random.fold_in(own, 1), rows)]
    turn = jax.random.randint(jax.random.fold_in(own, 2), (rows, 1), 0, top)
    return jnp.take_along_axis(grid, (jnp.arange(top)[None, :] + turn) % top, axis=1)


def load_shares(number_of, total, most, lean, full):
    weights = [(1 << 20) // math.isqrt(standing ** lean) + 1 for standing in range(1, number_of + 1)]
    largest = most if full else min(most, max(-(-total // number_of), total * weights[0] // sum(weights)))
    least = 1 if total - largest >= number_of - 1 else 0
    given, spare = [largest] + [least] * (number_of - 1), total - largest - least * (number_of - 1)
    while spare > 0:
        movable = [i for i in range(1, number_of) if given[i] < largest] or [i for i in range(1, number_of) if given[i] < most]
        mass, left = sum([weights[i] for i in movable]), spare
        for i in movable:
            more = min(most - given[i], max(1, left * weights[i] // mass), spare)
            given[i] = given[i] + more
            spare = spare - more
    return np.array(given)


def bell_draw(rng, extent, width, bound, shards=(), held_as=jnp.bfloat16):
    level = block_levels(rng, extent, shards, -0.22, 0.18) if shards else 1.0
    result = jax.random.normal(rng, extent, jnp.float32) * width * level
    return jnp.minimum(jnp.maximum(result, -bound), bound).astype(held_as)


def setup_inputs(seed: int = 0) -> dict:
    arg_keys = jax.random.split(jax.random.key(seed), 10)
    tokens = bell_draw(arg_keys[0], (TOKENS, D), 1.0, 6.0, ((0, 32),))
    cotangent = draw_cotangent(jax.random.fold_in(arg_keys[9], 71), 0)
    routes_keys = jax.random.split(jax.random.fold_in(arg_keys[2], 1), TOKENS // TOK_DEV)
    routes_turns = jax.random.permutation(jax.random.fold_in(arg_keys[2], 3), TOKENS // TOK_DEV)
    routes = jax.vmap(lambda own, number: shared_out(jax.random.fold_in(arg_keys[2], 2), own, number, TOK_DEV, EXPERTS, TOP, CAP, 3))(routes_keys, routes_turns).reshape((TOKENS, TOP))
    route_weights = draw_route_weights(jax.random.fold_in(arg_keys[9], 71), 0)
    gate_weight = bell_draw(arg_keys[4], (EXPERTS * F, D), D ** -0.5, 0.09375, ((0, 256),))
    up_weight = bell_draw(arg_keys[5], (EXPERTS * F, D), D ** -0.5, 0.09375, ((0, 256),))
    down_weight = bell_draw(arg_keys[6], (EXPERTS * F, D), 1.0, 6.0, ((0, 256),))
    cluster = draw_cluster(jax.random.fold_in(arg_keys[9], 71), 0)
    merged_slot = jax.random.permutation(arg_keys[8], MERGED).astype(jnp.int32)
    return dict(tokens=tokens, cotangent=cotangent, routes=routes, route_weights=route_weights, gate_weight=gate_weight, up_weight=up_weight, down_weight=down_weight, cluster=cluster, merged_slot=merged_slot)


PRIOR = 0.1


def rounded(values):
    narrow = values.astype(jnp.bfloat16)
    narrow = lax.optimization_barrier(narrow)
    return narrow.astype(jnp.float32)


def reference(tokens, cotangent, routes, route_weights, gate_weight, up_weight, down_weight, cluster, merged_slot):
    group_size = EXPERTS // N_EXPERT
    token_wide = tokens.astype(jnp.float32).reshape(N_HIDDEN, TOK_DEV, D)
    cot_wide = cotangent.astype(jnp.float32).reshape(N_HIDDEN, TOK_DEV, D)
    route_blocks = routes.reshape(N_HIDDEN, TOK_DEV, TOP)
    weight_blocks = route_weights.reshape(N_HIDDEN, TOK_DEV, TOP)
    merged_ids = jnp.arange(MERGED, dtype=jnp.int32)
    slot_table = jnp.sum(jnp.where(cluster[:, None] == merged_ids[None, :], merged_slot[None, :], 0), axis=1)
    places_all = jnp.arange(CAP, dtype=jnp.int32)
    expert_ids = jnp.arange(EXPERTS, dtype=jnp.int32)

    def expert_terms(expert):
        matches = route_blocks == expert
        marked = jnp.any(matches, axis=2).astype(jnp.int32)
        places = jnp.cumsum(marked, axis=1) - marked
        slot_weight = jnp.sum(jnp.where(matches, weight_blocks, 0.0), axis=2)
        chosen = (marked[:, None, :] == 1) & (places[:, None, :] == places_all[None, :, None])
        picker = jnp.where(chosen, 1.0, 0.0).astype(jnp.float32)
        token_rows = jnp.einsum("hct,htd->hcd", picker, token_wide).astype(jnp.bfloat16).reshape(N_HIDDEN * CAP, D)
        cot_rows = jnp.einsum("hct,htd->hcd", picker, cot_wide)
        scales = jnp.sum(picker * slot_weight[:, None, :], axis=2)
        grad_rows = (scales[:, :, None] * cot_rows).astype(jnp.bfloat16).reshape(N_HIDDEN * CAP, D)
        start = (expert * F).astype(jnp.int32)
        gate_rows = lax.dynamic_slice_in_dim(gate_weight, start, F, 0)
        up_rows = lax.dynamic_slice_in_dim(up_weight, start, F, 0)
        down_rows = lax.dynamic_slice_in_dim(down_weight, start, F, 0)
        dims = (((1,), (1,)), ((), ()))
        gate_value = lax.dot_general(token_rows, gate_rows, dims, preferred_element_type=jnp.float32)
        up_value = lax.dot_general(token_rows, up_rows, dims, preferred_element_type=jnp.float32)
        hidden_act = jax.nn.silu(gate_value) * up_value
        hidden_sq = (hidden_act * hidden_act).astype(jnp.bfloat16)
        grad_wide = grad_rows.astype(jnp.float32)
        grad_sq = (grad_wide * grad_wide).astype(jnp.bfloat16)
        fisher = jnp.dot(hidden_sq.T, grad_sq, preferred_element_type=jnp.float32)
        weighting = fisher + PRIOR
        numer = (weighting * down_rows.astype(jnp.float32)).astype(jnp.bfloat16)
        denom = weighting.astype(jnp.bfloat16)
        return numer, denom

    def group_step(carry, group_id):
        members = group_id * group_size + jnp.arange(group_size, dtype=jnp.int32)
        numer, denom = lax.map(expert_terms, members)
        member_slots = jnp.sum(jnp.where(members[:, None] == expert_ids[None, :], slot_table[None, :], 0), axis=1)
        mixer = jnp.where(member_slots[None, :] == merged_ids[:, None], 1.0, 0.0).astype(jnp.float32)
        numer_part = jnp.einsum("me,efd->mfd", mixer, numer.astype(jnp.float32))
        denom_part = jnp.einsum("me,efd->mfd", mixer, denom.astype(jnp.float32))
        return (carry[0] + rounded(numer_part), carry[1] + rounded(denom_part)), None

    zeros = jnp.zeros((MERGED, F, D), jnp.float32)
    totals, _ = lax.scan(group_step, (zeros, zeros), jnp.arange(N_EXPERT, dtype=jnp.int32))
    merged = (totals[0] / totals[1]).astype(jnp.bfloat16)
    return merged.reshape(MERGED, SLICE_COUNT, SLICE_ROWS, D)
```

```python
import jax
import jax.numpy as jnp
from jax import lax
from jax.sharding import Mesh, PartitionSpec as P

F = 1024
EXPERTS = 64
MERGED = 24
CAP = 20
PRIOR = 0.1
NY, NC, NZ, NX = 4, 2, 8, 4
OWN = MERGED // (NY * NC)


bf16 = jnp.bfloat16
f32 = jnp.float32


def shift(a, axis, size, step):
    return lax.ppermute(a, axis, [(i, (i + step) % size) for i in range(size)])


def slot_lookup(cluster, merged_slot):
    ids = jnp.arange(MERGED, dtype=jnp.int32)
    return jnp.sum(jnp.where(cluster[:, None] == ids[None, :], merged_slot[None, :], 0), axis=1)


def pick_tables(routes, route_weights, first_expert):
    members = first_expert + jnp.arange(NZ, dtype=jnp.int32)
    matches = routes[:, :, None] == members[None, None, :]
    marked = jnp.any(matches, axis=1).astype(jnp.int32)
    places = jnp.cumsum(marked, axis=0) - marked
    slot_weight = jnp.sum(jnp.where(matches, route_weights[:, :, None], 0.0), axis=1)
    places_all = jnp.arange(CAP, dtype=jnp.int32)
    chosen = (marked.T[:, None, :] == 1) & (places.T[:, None, :] == places_all[None, :, None])
    picker = chosen.astype(bf16).reshape(NZ * CAP, routes.shape[0])
    scales = jnp.sum(jnp.where(chosen, slot_weight.T[:, None, :], 0.0), axis=2)
    return picker, scales.reshape(NZ * CAP, 1)


def ring_x(block):
    half = block.shape[0] // 2
    right = shift(block, "x", NX, 1)
    left = shift(block, "x", NX, -1)
    far_a = shift(right[:half], "x", NX, 1)
    far_b = shift(left[half:], "x", NX, -1)
    return block, right, left, far_a, far_b


def square_hidden(rows, gate, up):
    dims = (((1,), (1,)), ((), ()))
    g = lax.dot_general(rows, gate, dims, preferred_element_type=f32)
    u = lax.dot_general(rows, up, dims, preferred_element_type=f32)
    h = jax.nn.silu(g) * u
    return (h * h).astype(bf16)


def square(rows):
    wide = rows.astype(f32)
    return (wide * wide).astype(bf16)


def ring_reduce_y(parts):
    half = parts.shape[1] // 2
    up = shift(parts[2][:half], "y", NY, 1)
    down = shift(parts[2][half:], "y", NY, -1)
    one = jnp.concatenate([parts[1][:half].astype(f32) + up.astype(f32), parts[1][half:].astype(f32)])
    three = jnp.concatenate([parts[3][:half].astype(f32), parts[3][half:].astype(f32) + down.astype(f32)])
    got_up = shift(one.astype(bf16), "y", NY, 1)
    got_down = shift(three.astype(bf16), "y", NY, -1)
    return parts[0].astype(f32) + got_up.astype(f32) + got_down.astype(f32)


def per_device(tokens, cotangent, routes, route_weights, gate, up, down, cluster, merged_slot):
    width = gate.shape[1]
    y, c = lax.axis_index("y"), lax.axis_index("c")
    group = y * NC + c
    first_expert = group * NZ
    picker, scales = pick_tables(routes, route_weights, first_expert)
    token_rows = jnp.dot(picker, tokens, preferred_element_type=f32).astype(bf16)
    cot_rows = jnp.dot(picker, cotangent, preferred_element_type=f32)
    grad_rows = (scales * cot_rows).astype(bf16)

    def over_z(rows):
        got = lax.all_to_all(rows.reshape(NZ, CAP, width), "z", 0, 0, tiled=True)
        return got.reshape(NZ * CAP, width)

    token_mine = over_z(token_rows)
    grad_mine = over_z(grad_rows)
    token_parts = ring_x(token_mine)
    grad_parts = ring_x(grad_mine)
    down_recv = lax.all_to_all(down, ("z", "x"), 0, 0, tiled=True)

    def join(parts):
        return parts[0], jnp.concatenate(parts[1:3]), jnp.concatenate(parts[3:5])

    fisher = None
    for trows, grows in zip(join(token_parts), join(grad_parts)):
        hs = square_hidden(trows, gate, up)
        part = lax.dot_general(hs, square(grows), (((0,), (0,)), ((), ())), preferred_element_type=f32)
        fisher = part if fisher is None else fisher + part
    denom = (fisher + PRIOR).astype(bf16)
    denom_recv = lax.all_to_all(denom, ("z", "x"), 0, 0, tiled=True)

    den = denom_recv.reshape(NZ, NX * 8 * width)
    num = (denom_recv.astype(f32) * down_recv.astype(f32)).astype(bf16).reshape(NZ, NX * 8 * width)
    slot_table = slot_lookup(cluster, merged_slot)
    expert_ids = jnp.arange(EXPERTS, dtype=jnp.int32)
    member = first_expert + jnp.arange(NZ, dtype=jnp.int32)
    member_slot = jnp.sum(jnp.where(member[:, None] == expert_ids[None, :], slot_table[None, :], 0), axis=1)

    def mixed(core, block):
        owner = ((y + jnp.arange(NY, dtype=jnp.int32)) % NY) * NC + core
        slots = (owner[:, None] * OWN + jnp.arange(OWN, dtype=jnp.int32)[None, :]).reshape(-1)
        mix = (slots[:, None] == member_slot[None, :]).astype(bf16)
        return jnp.dot(mix, block, preferred_element_type=f32).astype(bf16)

    totals = []
    for block in (num, den):
        other = shift(mixed(1 - c, block), "c", NC, 1)
        mine = mixed(c, block)
        both = (mine.astype(f32) + other.astype(f32)).astype(bf16)
        totals.append(ring_reduce_y(both.reshape(NY, OWN * NX * 8, width)))
    return (totals[0] / totals[1]).astype(bf16).reshape(OWN, NX, 8, width)


def solution(mesh):
    fine = Mesh(mesh.devices.reshape(NY, NC, NZ, NX), ("y", "c", "z", "x"))
    rows = P(("z", "x"), None)
    units = P(("y", "c", "z", "x"), None)
    return jax.shard_map(
        per_device,
        mesh=fine,
        in_specs=(rows, rows, rows, rows, units, units, units, P(), P()),
        out_specs=P(("y", "c"), None, ("z", "x"), None),
        check_vma=False,
    )
```

```python
import functools

import jax
import jax.numpy as jnp
from jax import lax
from jax.experimental import pallas as pl
from jax.experimental.pallas import tpu as pltpu
from jax.sharding import Mesh, PartitionSpec as P


F = 1024
EXPERTS = 64
MERGED = 24
CAP = 20
PRIOR = 0.1
NY, NC, NZ, NX = 4, 2, 8, 4
OWN = MERGED // (NY * NC)
ROWS = NZ * CAP
PIECE = F // (NZ * NX * NX)
HALVES = ((0, 1), (3, 2))
ORDER = (0, 1, 3)
HOPS = (1, 3, 0)
INTERPRET = False


bf16 = jnp.bfloat16
f32 = jnp.float32


def shift(a, axis, size, step):
    return lax.ppermute(a, axis, [(i, (i + step) % size) for i in range(size)])


def slot_lookup(cluster, merged_slot):
    ids = jnp.arange(MERGED, dtype=jnp.int32)
    return jnp.sum(jnp.where(cluster[:, None] == ids[None, :], merged_slot[None, :], 0), axis=1)


def pick_tables(routes, route_weights, first_expert):
    members = first_expert + jnp.arange(NZ, dtype=jnp.int32)
    matches = routes[:, :, None] == members[None, None, :]
    marked = jnp.any(matches, axis=1).astype(jnp.int32)
    places = jnp.cumsum(marked, axis=0) - marked
    slot_weight = jnp.sum(jnp.where(matches, route_weights[:, :, None], 0.0), axis=1)
    places_all = jnp.arange(CAP, dtype=jnp.int32)
    chosen = (marked.T[:, None, :] == 1) & (places.T[:, None, :] == places_all[None, :, None])
    picker = chosen.astype(bf16).reshape(ROWS, routes.shape[0])
    scales = jnp.sum(jnp.where(chosen, slot_weight.T[:, None, :], 0.0), axis=2)
    return picker, scales.reshape(ROWS, 1)


def hidden_kernel(*refs, pieces):
    blocks, gate_ref, up_ref, out_ref, acc_ref = refs[:pieces], *refs[pieces:]
    step = pl.program_id(0)
    rows = jnp.concatenate([b[...] for b in blocks], axis=0)
    units = gate_ref.shape[0]
    dims = (((1,), (1,)), ((), ()))
    g = lax.dot_general(rows, gate_ref[...], dims, preferred_element_type=f32)
    u = lax.dot_general(rows, up_ref[...], dims, preferred_element_type=f32)

    @pl.when(step == 0)
    def _():
        acc_ref[:, :units] = g
        acc_ref[:, units:] = u

    @pl.when(step > 0)
    def _():
        acc_ref[:, :units] += g
        acc_ref[:, units:] += u

    @pl.when(step == pl.num_programs(0) - 1)
    def _():
        gv = acc_ref[:, :units]
        h = gv / (1.0 + jnp.exp(-gv)) * acc_ref[:, units:]
        out_ref[...] = (h * h).astype(bf16)


def hidden(pieces, gate, up):
    width = gate.shape[1]
    units = gate.shape[0]
    step = width // NX
    total = sum(p.shape[0] for p in pieces)
    col = lambda k: (0, k)
    return pl.pallas_call(
        functools.partial(hidden_kernel, pieces=len(pieces)),
        grid=(NX,),
        in_specs=[pl.BlockSpec((p.shape[0], step), col) for p in pieces]
        + [pl.BlockSpec((units, step), col)] * 2,
        out_specs=pl.BlockSpec((total, units), lambda k: (0, 0)),
        out_shape=jax.ShapeDtypeStruct((total, units), bf16),
        scratch_shapes=[pltpu.VMEM((total, 2 * units), f32)],
        interpret=INTERPRET,
        name="hidden",
    )(*pieces, gate, up)


def fisher_kernel(ha_ref, hb_ref, la_ref, lb_ref, g_ref, out_ref, *, half):
    for j, (early, late) in enumerate(((ha_ref, la_ref), (hb_ref, lb_ref))):
        e = half[j]
        h = jnp.concatenate([early[...], late[...]], axis=0)
        g = jnp.concatenate([g_ref[(e + d) % NX] for d in ORDER + (2,)], axis=0)
        acc = lax.dot_general(h, g, (((0,), (0,)), ((), ())), preferred_element_type=f32)
        acc = acc + PRIOR
        out_ref[:, j * PIECE : (j + 1) * PIECE, :] = acc.reshape(NZ * NX, PIECE, -1).astype(bf16)


def fisher_half(half, early, late, grad_sq):
    a, b = half
    return pl.pallas_call(
        functools.partial(fisher_kernel, half=half),
        out_shape=jax.ShapeDtypeStruct((NZ * NX, 2 * PIECE, grad_sq.shape[-1]), bf16),
        interpret=INTERPRET,
        name="fisher",
    )(early[a], early[b], late[a], late[b], grad_sq)


def mix_kernel(kron_ref, den_ref, da_ref, db_ref, *refs):
    snd2_ref, snd_ref, own2_ref, own_ref = refs[-4:]
    mix = kron_ref[...]
    block = OWN * PIECE
    for j, down_ref in enumerate((da_ref, db_ref)):
        den = den_ref[:, 0, j * PIECE : (j + 1) * PIECE, :].astype(f32)
        num = den * down_ref[:, 0].astype(f32)
        for arr, val in enumerate((num, den)):
            flat = val.reshape(NZ * PIECE, -1).astype(bf16)
            res = jnp.dot(mix, flat, preferred_element_type=f32).astype(bf16)
            rows = slice(j * block, (j + 1) * block)
            for core, (two, rest) in enumerate(((own2_ref, own_ref), (snd2_ref, snd_ref))):
                base = core * NY * block
                two[arr, rows, :] = res[base + 2 * block : base + 3 * block]
                for n, hop in enumerate(HOPS):
                    rest[arr, n, rows, :] = res[base + hop * block : base + (hop + 1) * block]


def mix(half, kron, den, down, after):
    chunk = den.shape[-1]
    width = down.shape[-1]
    tall = 2 * OWN * PIECE
    two = jax.ShapeDtypeStruct((2, tall, width), bf16)
    rest = jax.ShapeDtypeStruct((2, len(HOPS), tall, width), bf16)
    two_spec = pl.BlockSpec((2, tall, chunk), lambda k: (0, 0, k))
    rest_spec = pl.BlockSpec((2, len(HOPS), tall, chunk), lambda k: (0, 0, 0, k))

    def down_spec(e):
        return pl.BlockSpec((NZ, 1, PIECE, chunk), lambda k: (0, lax.rem(k + e, NX), 0, k))

    return pl.pallas_call(
        mix_kernel,
        grid=(NX,),
        in_specs=[
            pl.BlockSpec(kron.shape, lambda k: (0, 0)),
            pl.BlockSpec((NZ, 1, 2 * PIECE, chunk), lambda k: (0, k, 0, 0)),
            down_spec(half[0]),
            down_spec(half[1]),
        ]
        + [pl.BlockSpec(memory_space=pl.ANY)] * len(after),
        out_specs=[two_spec, rest_spec, two_spec, rest_spec],
        out_shape=[two, rest, two, rest],
        interpret=INTERPRET,
        name="mix",
    )(kron, den.reshape(NZ, NX, 2 * PIECE, chunk), down, down, *after)


def final_kernel(*refs):
    out_ref = refs[-1]
    block = OWN * PIECE
    k = pl.program_id(0)
    for n, half in enumerate(HALVES):
        own, oth, up_num, up_den, dn_num, dn_den = refs[6 * n : 6 * n + 6]
        tot = []
        for arr, up, dn in ((0, up_num, dn_num), (1, up_den, dn_den)):
            tot.append(
                own[arr, 0].astype(f32) + oth[arr, 0].astype(f32) + up[...].astype(f32) + dn[...].astype(f32)
            )
        res = (tot[0] / tot[1]).astype(bf16)
        for j, e in enumerate(half):
            s = lax.rem(k + e, NX)
            for m in range(OWN):
                out_ref[m, s] = res[j * block + m * PIECE : j * block + (m + 1) * PIECE]


def final(groups):
    tall, width = groups[0][2].shape
    chunk = width // NX
    flat = pl.BlockSpec((tall, chunk), lambda k: (0, k))
    rest = pl.BlockSpec((2, 1, tall, chunk), lambda k: (0, 2, 0, k))
    return pl.pallas_call(
        final_kernel,
        grid=(NX,),
        in_specs=[rest, rest, flat, flat, flat, flat] * 2,
        out_specs=pl.BlockSpec((OWN, NX, PIECE, chunk), lambda k: (0, 0, 0, k)),
        out_shape=jax.ShapeDtypeStruct((OWN, NX, PIECE, width), bf16),
        interpret=INTERPRET,
        name="final",
    )(*groups[0], *groups[1])


def add(*parts):
    total = parts[0].astype(f32)
    for p in parts[1:]:
        total = total + p.astype(f32)
    return total.astype(bf16)


def reduce_slots(snd2, snd, own2, own):
    oth2 = shift(snd2, "c", NC, 1)
    oth = shift(snd, "c", NC, 1)
    two_num = add(own2[0], oth2[0])
    two_den = add(own2[1], oth2[1])
    one_den = add(own[1, 0], oth[1, 0])
    three_num = add(own[0, 1], oth[0, 1])
    up1 = shift(two_num, "y", NY, 1)
    dn1 = shift(two_den, "y", NY, -1)
    up_den = shift(one_den, "y", NY, 1)
    dn_num = shift(three_num, "y", NY, -1)
    one_num = add(own[0, 0], oth[0, 0], up1)
    three_den = add(own[1, 1], oth[1, 1], dn1)
    up_num = shift(one_num, "y", NY, 1)
    dn_den = shift(three_den, "y", NY, -1)
    return (own, oth, up_num, up_den, dn_num, dn_den), (one_num, three_den)


def per_device(tokens, cotangent, routes, route_weights, gate, up, down, cluster, merged_slot):
    width = gate.shape[1]
    chunk = width // NX
    y, c, x = lax.axis_index("y"), lax.axis_index("c"), lax.axis_index("x")
    first_expert = (y * NC + c) * NZ
    picker, scales = pick_tables(routes, route_weights, first_expert)
    token_rows = jnp.dot(picker, tokens, preferred_element_type=f32).astype(bf16)
    got = lax.all_to_all(token_rows.reshape(NZ, CAP, width), "z", 0, 0, tiled=True)
    part_a = got[: NZ // 2].reshape(ROWS // 2, width)
    part_b = got[NZ // 2 :].reshape(ROWS // 2, width)
    right_a = shift(part_a, "x", NX, 1)
    left_b = shift(part_b, "x", NX, -1)
    right_b = shift(part_b, "x", NX, 1)
    left_a = shift(part_a, "x", NX, -1)
    far_a = shift(right_a, "x", NX, 1)
    far_b = shift(left_b, "x", NX, -1)

    cot_rows = jnp.dot(picker, cotangent, preferred_element_type=f32)
    grad_rows = (scales * cot_rows).astype(bf16)
    grad_send = grad_rows.reshape(NZ, CAP, NX, chunk).transpose(0, 2, 1, 3)
    grad_send = grad_send.reshape(NZ * NX, CAP, chunk)
    grad_recv = lax.all_to_all(grad_send, ("z", "x"), 0, 0, tiled=True)
    grad_abs = grad_recv.reshape(NZ, NX, CAP, chunk).transpose(1, 0, 2, 3).reshape(NX, ROWS, chunk)
    wide = grad_abs.astype(f32)
    square = (wide * wide).astype(bf16)
    grad_sq = lax.dynamic_slice_in_dim(jnp.concatenate([square, square]), x, NX, 0)

    down_recv = lax.all_to_all(down, ("z", "x"), 0, 0, tiled=True)
    down_recv = down_recv.reshape(NZ, NX, PIECE, width)

    h_own = hidden((part_a, part_b), gate, up)
    h_near = hidden((left_a, left_b, right_a, right_b), gate, up)
    early0 = jnp.concatenate([h_own, h_near])
    late0 = hidden((far_a, far_b), gate, up)
    early = {0: early0}
    late = {0: late0}
    for e in (1, 3, 2):
        early[e] = shift(early0, "x", NX, -e)
        late[e] = shift(late0, "x", NX, -e)

    slot_table = slot_lookup(cluster, merged_slot)
    expert_ids = jnp.arange(EXPERTS, dtype=jnp.int32)
    member = first_expert + jnp.arange(NZ, dtype=jnp.int32)
    member_slot = jnp.sum(
        jnp.where(member[:, None] == expert_ids[None, :], slot_table[None, :], 0), axis=1
    )
    owner_core = (c + jnp.arange(NC, dtype=jnp.int32)) % NC
    owner_y = (y + jnp.arange(NY, dtype=jnp.int32)) % NY
    owner = owner_y[None, :] * NC + owner_core[:, None]
    slots = (owner[:, :, None] * OWN + jnp.arange(OWN, dtype=jnp.int32)).reshape(-1)
    same_slot = jnp.repeat(slots, PIECE)[:, None] == jnp.repeat(member_slot, PIECE)[None, :]
    q_row = jnp.arange(MERGED * PIECE, dtype=jnp.int32)[:, None] % PIECE
    q_col = jnp.arange(NZ * PIECE, dtype=jnp.int32)[None, :] % PIECE
    kron = (same_slot & (q_row == q_col)).astype(bf16)

    groups = []
    after = ()
    for half in HALVES:
        denom = fisher_half(half, early, late, grad_sq)
        denom_recv = lax.all_to_all(denom, ("z", "x"), 0, 0, tiled=True)
        mixed = mix(half, kron, denom_recv, down_recv, after)
        group, after = reduce_slots(*mixed)
        groups.append(group)
    return final(groups)


def solution(mesh):
    fine = Mesh(mesh.devices.reshape(NY, NC, NZ, NX), ("y", "c", "z", "x"))
    rows = P(("z", "x"), None)
    units = P(("y", "c", "z", "x"), None)

    return jax.shard_map(
        per_device,
        mesh=fine,
        in_specs=(rows, rows, rows, rows, units, units, units, P(), P()),
        out_specs=P(("y", "c"), None, ("z", "x"), None),
        check_vma=False,
    )
```

```python
import functools

import jax
import jax.numpy as jnp
from jax import lax
from jax.experimental import pallas as pl
from jax.experimental.pallas import tpu as pltpu
from jax.sharding import Mesh, PartitionSpec as P


F = 1024
EXPERTS = 64
MERGED = 24
CAP = 20
PRIOR = 0.1
NY, NC, NZ, NX = 4, 2, 8, 4
OWN = MERGED // (NY * NC)
ROWS = NZ * CAP
TALL = 24
STEPS = (0, 1, 7, 2, 6, 3, 5, 4)
PIECE = F // (NZ * NX * NX)
HALVES = ((0, 1), (3, 2))
ORDER = (0, 1, 3)
HOPS = (1, 3, 0)
COLS = 7
INTERPRET = False


bf16 = jnp.bfloat16
f32 = jnp.float32


def shift(a, axis, size, step):
    return lax.ppermute(a, axis, [(i, (i + step) % size) for i in range(size)])


def slot_lookup(cluster, merged_slot):
    ids = jnp.arange(MERGED, dtype=jnp.int32)
    return jnp.sum(jnp.where(cluster[:, None] == ids[None, :], merged_slot[None, :], 0), axis=1)


def pick_tables(routes, route_weights, members):
    matches = routes[:, :, None] == members[None, None, :]
    marked = jnp.any(matches, axis=1).astype(jnp.int32)
    places = jnp.cumsum(marked, axis=0) - marked
    slot_weight = jnp.sum(jnp.where(matches, route_weights[:, :, None], 0.0), axis=1)
    places_all = jnp.arange(TALL, dtype=jnp.int32)
    chosen = (marked.T[:, None, :] == 1) & (places.T[:, None, :] == places_all[None, :, None])
    weights = jnp.where(chosen, slot_weight.T[:, None, :], 0.0)
    shape = (NZ * TALL, routes.shape[0])
    return chosen.astype(bf16).reshape(shape), weights.reshape(shape)


def pack_kernel(pick_ref, high_ref, low_ref, turn_ref, tok_ref, *outs):
    width = tok_ref.shape[1]
    step = width // COLS

    def body(k, carry):
        cols = pl.ds(pl.multiple_of(k * step, step), step)
        rows = jnp.dot(pick_ref[...], tok_ref[:, cols], preferred_element_type=f32).astype(bf16)
        for n, out in enumerate(outs):
            out[:, cols] = rows[n * TALL : n * TALL + CAP]
        return carry

    lax.fori_loop(0, COLS, body, 0)
    high = jnp.dot(high_ref[...], turn_ref[...], preferred_element_type=f32)
    low = jnp.dot(low_ref[...], turn_ref[...], preferred_element_type=f32)
    tail = jnp.concatenate([high, low], axis=1).astype(bf16)
    for n, out in enumerate(outs):
        out[:, width:] = tail[n * TALL : n * TALL + CAP]


def pack(pick, weights, turn, tokens):
    high = weights.astype(bf16)
    low = (weights - high.astype(f32)).astype(bf16)
    shape = jax.ShapeDtypeStruct((CAP, tokens.shape[1] + 2 * tokens.shape[0]), bf16)
    return pl.pallas_call(
        pack_kernel,
        out_shape=[shape] * NZ,
        interpret=INTERPRET,
        name="pack",
    )(pick, high, low, turn, tokens)


def pick_kernel(src_ref, spread_ref, *refs):
    tails, cots, out_ref, tail_ref = refs[: 2 * NX], refs[2 * NX : -2], refs[-2], refs[-1]
    group = NZ // 2
    height = group * CAP
    per = cots[0].shape[2]
    tok = per * len(cots)
    row = lax.broadcasted_iota(jnp.int32, (height, group * tok), 0) // CAP
    col = lax.broadcasted_iota(jnp.int32, (height, group * tok), 1) // tok
    same = row == col
    for n, t in enumerate(tails):
        tail_ref[n] = t[...]

    def body(n, carry):
        half = n % 2
        xs = src_ref[NZ + n // 2]
        wide = jnp.dot(tail_ref[n], spread_ref[...], preferred_element_type=f32)
        high = jnp.where(same, wide[:, : group * tok], 0.0).astype(bf16)
        low = jnp.where(same, wide[:, group * tok :], 0.0).astype(bf16)
        blocks = []
        for j in range(group):
            zs = src_ref[half * group + j]
            blocks += [cot[zs, xs].astype(f32) for cot in cots]
        cot = jnp.concatenate(blocks, axis=0).astype(bf16)
        val = jnp.dot(high, cot, preferred_element_type=f32)
        val = val + jnp.dot(low, cot, preferred_element_type=f32)
        val = val.astype(bf16).astype(f32)
        out_ref[n] = (val * val).astype(bf16)
        return carry

    lax.fori_loop(0, 2 * NX, body, 0)


def pick(sources, spread, pieces, cots, width):
    lanes = spread.shape[0]
    height = pieces[0].shape[0]
    chunk = cots[0].shape[-1]
    tail = pl.BlockSpec((height, lanes), lambda i, src: (0, width // lanes))
    whole = lambda a: pl.BlockSpec(a.shape, lambda i, src: (0,) * a.ndim)
    return pl.pallas_call(
        pick_kernel,
        grid_spec=pltpu.PrefetchScalarGridSpec(
            num_scalar_prefetch=1,
            grid=(1,),
            in_specs=[whole(spread)] + [tail] * len(pieces) + [whole(c) for c in cots],
            out_specs=pl.BlockSpec((2 * NX, ROWS // 2, chunk), lambda i, src: (0, 0, 0)),
            scratch_shapes=[pltpu.VMEM((2 * NX, height, lanes), bf16)],
        ),
        out_shape=jax.ShapeDtypeStruct((2 * NX, ROWS // 2, chunk), bf16),
        interpret=INTERPRET,
        name="pick",
    )(sources, spread, *pieces, *cots).reshape(NX, ROWS, chunk)


def hidden_kernel(*refs, pieces):
    blocks, gate_ref, up_ref, out_ref, acc_ref = refs[:pieces], *refs[pieces:]
    step = pl.program_id(0)
    rows = jnp.concatenate([b[...] for b in blocks], axis=0)
    units = gate_ref.shape[0]
    dims = (((1,), (1,)), ((), ()))
    g = lax.dot_general(rows, gate_ref[...], dims, preferred_element_type=f32)
    u = lax.dot_general(rows, up_ref[...], dims, preferred_element_type=f32)

    @pl.when(step == 0)
    def _():
        acc_ref[:, :units] = g
        acc_ref[:, units:] = u

    @pl.when(step > 0)
    def _():
        acc_ref[:, :units] += g
        acc_ref[:, units:] += u

    @pl.when(step == pl.num_programs(0) - 1)
    def _():
        gv = acc_ref[:, :units]
        h = gv / (1.0 + jnp.exp(-gv)) * acc_ref[:, units:]
        out_ref[...] = (h * h).astype(bf16)


def hidden(pieces, gate, up):
    width = gate.shape[1]
    units = gate.shape[0]
    step = width // COLS
    total = sum(p.shape[0] for p in pieces)
    col = lambda k: (0, k)
    return pl.pallas_call(
        functools.partial(hidden_kernel, pieces=len(pieces)),
        grid=(COLS,),
        in_specs=[pl.BlockSpec((p.shape[0], step), col) for p in pieces]
        + [pl.BlockSpec((units, step), col)] * 2,
        out_specs=pl.BlockSpec((total, units), lambda k: (0, 0)),
        out_shape=jax.ShapeDtypeStruct((total, units), bf16),
        scratch_shapes=[pltpu.VMEM((total, 2 * units), f32)],
        interpret=INTERPRET,
        name="hidden",
    )(*pieces, gate, up)


def fisher_kernel(ha_ref, hb_ref, la_ref, lb_ref, g_ref, out_ref, *, half):
    for j, (early, late) in enumerate(((ha_ref, la_ref), (hb_ref, lb_ref))):
        e = half[j]
        h = jnp.concatenate([early[...], late[...]], axis=0)
        g = jnp.concatenate([g_ref[(e + d) % NX] for d in ORDER + (2,)], axis=0)
        acc = lax.dot_general(h, g, (((0,), (0,)), ((), ())), preferred_element_type=f32)
        acc = acc + PRIOR
        out_ref[:, j * PIECE : (j + 1) * PIECE, :] = acc.reshape(-1, PIECE, acc.shape[1]).astype(bf16)


def fisher_half(half, early, late, grad_sq):
    a, b = half
    units = early[a].shape[1] // 2
    chunk = grad_sq.shape[-1]
    hid = lambda h: pl.BlockSpec((h.shape[0], units), lambda k: (0, k))
    return pl.pallas_call(
        functools.partial(fisher_kernel, half=half),
        grid=(2,),
        in_specs=[hid(early[a]), hid(early[b]), hid(late[a]), hid(late[b])]
        + [pl.BlockSpec(grad_sq.shape, lambda k: (0, 0, 0))],
        out_specs=pl.BlockSpec((NZ * NX // 2, 2 * PIECE, chunk), lambda k: (k, 0, 0)),
        out_shape=jax.ShapeDtypeStruct((NZ * NX, 2 * PIECE, grad_sq.shape[-1]), bf16),
        interpret=INTERPRET,
        name="fisher",
    )(early[a], early[b], late[a], late[b], grad_sq)


def mix_kernel(kron_ref, den_ref, da_ref, db_ref, *refs):
    snd2_ref, snd_ref, own2_ref, own_ref, val_ref = refs[-5:]
    mix = kron_ref[...]
    block = OWN * PIECE
    for j, down_ref in enumerate((da_ref, db_ref)):
        den_all = den_ref[:, 0, j * PIECE : (j + 1) * PIECE, :].astype(f32)
        num_all = den_all * down_ref[:, 0].astype(f32)
        val_ref[2 * j] = num_all.reshape(NZ * PIECE, -1).astype(bf16)
        val_ref[2 * j + 1] = den_all.reshape(NZ * PIECE, -1).astype(bf16)

    def body(n, carry):
        arr = n % 2
        rows = pl.ds(pl.multiple_of(n // 2 * block, PIECE), block)
        res = jnp.dot(mix, val_ref[n], preferred_element_type=f32).astype(bf16)
        for core, (two, rest) in enumerate(((own2_ref, own_ref), (snd2_ref, snd_ref))):
            base = core * NY * block
            two[arr, rows, :] = res[base + 2 * block : base + 3 * block]
            for i, hop in enumerate(HOPS):
                rest[arr, i, rows, :] = res[base + hop * block : base + (hop + 1) * block]
        return carry

    lax.fori_loop(0, 4, body, 0)


def mix(half, kron, den, down, after):
    chunk = den.shape[-1]
    width = down.shape[-1]
    tall = 2 * OWN * PIECE
    two = jax.ShapeDtypeStruct((2, tall, width), bf16)
    rest = jax.ShapeDtypeStruct((2, len(HOPS), tall, width), bf16)
    two_spec = pl.BlockSpec((2, tall, chunk), lambda k: (0, 0, k))
    rest_spec = pl.BlockSpec((2, len(HOPS), tall, chunk), lambda k: (0, 0, 0, k))

    def down_spec(e):
        return pl.BlockSpec((NZ, 1, PIECE, chunk), lambda k: (0, lax.rem(k + e, NX), 0, k))

    return pl.pallas_call(
        mix_kernel,
        grid=(NX,),
        in_specs=[
            pl.BlockSpec(kron.shape, lambda k: (0, 0)),
            pl.BlockSpec((NZ, 1, 2 * PIECE, chunk), lambda k: (0, k, 0, 0)),
            down_spec(half[0]),
            down_spec(half[1]),
        ]
        + [pl.BlockSpec(memory_space=pl.ANY)] * len(after),
        out_specs=[two_spec, rest_spec, two_spec, rest_spec],
        out_shape=[two, rest, two, rest],
        scratch_shapes=[pltpu.VMEM((4, NZ * PIECE, chunk), bf16)],
        interpret=INTERPRET,
        name="mix",
    )(kron, den.reshape(NZ, NX, 2 * PIECE, chunk), down, down, *after)


def final_kernel(*refs):
    out_ref = refs[-1]
    block = OWN * PIECE
    k = pl.program_id(0)
    for n, half in enumerate(HALVES):
        own, oth, up_num, up_den, dn_num, dn_den = refs[6 * n : 6 * n + 6]
        tot = []
        for arr, up, dn in ((0, up_num, dn_num), (1, up_den, dn_den)):
            tot.append(
                own[arr, 0].astype(f32) + oth[arr, 0].astype(f32) + up[...].astype(f32) + dn[...].astype(f32)
            )
        res = (tot[0] / tot[1]).astype(bf16)
        for j, e in enumerate(half):
            s = lax.rem(k + e, NX)
            for m in range(OWN):
                out_ref[m, s] = res[j * block + m * PIECE : j * block + (m + 1) * PIECE]


def final(groups):
    tall, width = groups[0][2].shape
    chunk = width // NX
    flat = pl.BlockSpec((tall, chunk), lambda k: (0, k))
    rest = pl.BlockSpec((2, 1, tall, chunk), lambda k: (0, 2, 0, k))
    return pl.pallas_call(
        final_kernel,
        grid=(NX,),
        in_specs=[rest, rest, flat, flat, flat, flat] * 2,
        out_specs=pl.BlockSpec((OWN, NX, PIECE, chunk), lambda k: (0, 0, 0, k)),
        out_shape=jax.ShapeDtypeStruct((OWN, NX, PIECE, width), bf16),
        interpret=INTERPRET,
        name="final",
    )(*groups[0], *groups[1])


def add(*parts):
    total = parts[0].astype(f32)
    for p in parts[1:]:
        total = total + p.astype(f32)
    return total.astype(bf16)


def reduce_slots(snd2, snd, own2, own):
    oth2 = shift(snd2, "c", NC, 1)
    oth = shift(snd, "c", NC, 1)
    two_num = add(own2[0], oth2[0])
    two_den = add(own2[1], oth2[1])
    one_den = add(own[1, 0], oth[1, 0])
    three_num = add(own[0, 1], oth[0, 1])
    up1 = shift(two_num, "y", NY, 1)
    dn1 = shift(two_den, "y", NY, -1)
    up_den = shift(one_den, "y", NY, 1)
    dn_num = shift(three_num, "y", NY, -1)
    one_num = add(own[0, 0], oth[0, 0], up1)
    three_den = add(own[1, 1], oth[1, 1], dn1)
    up_num = shift(one_num, "y", NY, 1)
    dn_den = shift(three_den, "y", NY, -1)
    return (own, oth, up_num, up_den, dn_num, dn_den), (one_num, three_den)


def per_device(tokens, cotangent, routes, route_weights, gate, up, down, cluster, merged_slot):
    width = gate.shape[1]
    chunk = width // NX
    toks = tokens.shape[0]
    per = toks // (NY * NC)
    y, c = lax.axis_index("y"), lax.axis_index("c")
    z, x = lax.axis_index("z"), lax.axis_index("x")
    group = y * NC + c
    first_expert = group * NZ
    steps = jnp.array(STEPS, dtype=jnp.int32)
    picker, weights = pick_tables(routes, route_weights, first_expert + (z + steps) % NZ)
    place = jnp.arange(toks, dtype=jnp.int32)
    ahead, other, row = place // (NC * per), place // per % NC, place % per
    turned = (((y + ahead) % NY) * NC + (c + other) % NC) * per + row
    turn = (place[:, None] == turned[None, :]).astype(bf16)
    blocks = pack(picker, weights, turn, tokens)
    got = [blocks[0]]
    for n, step in enumerate(STEPS[1:]):
        got.append(shift(blocks[n + 1], "z", NZ, step))
    part_a = jnp.concatenate(got[: NZ // 2])
    part_b = jnp.concatenate(got[NZ // 2 :])
    right_a = shift(part_a, "x", NX, 1)
    left_a = shift(part_a, "x", NX, -1)
    left_b = shift(part_b, "x", NX, -1)
    right_b = shift(part_b, "x", NX, 1)
    far_a = shift(right_a, "x", NX, 1)
    far_b = shift(left_b, "x", NX, -1)

    cot_own = lax.dynamic_slice_in_dim(cotangent, group * per, per, 0)
    cot_own = cot_own.reshape(per, NX, chunk).transpose(1, 0, 2)
    cot_send = jnp.broadcast_to(cot_own[None], (NZ, NX, per, chunk)).reshape(NZ * NX, per, chunk)
    cot0 = lax.all_to_all(cot_send, ("z", "x"), 0, 0, tiled=True)
    cot3 = shift(cot0, "y", NY, 1)
    cot1 = shift(cot0, "y", NY, -1)
    half = NZ * NX // 2
    two_a = shift(cot3[:half], "y", NY, 1)
    two_b = shift(cot1[half:], "y", NY, -1)
    cot2 = jnp.concatenate([two_a, two_b])
    cots = []
    for a in (cot0, cot1, cot2, cot3):
        b = shift(a, "c", NC, 1)
        cots += [a.reshape(NZ, NX, per, chunk), b.reshape(NZ, NX, per, chunk)]
    sources = jnp.concatenate([(z - steps) % NZ, (x + jnp.arange(NX, dtype=jnp.int32)) % NX])
    lane = jnp.arange(2 * toks, dtype=jnp.int32)[:, None]
    wide = jnp.arange(NZ * toks, dtype=jnp.int32)[None, :]
    spread = ((lane % toks == wide % toks) & (lane // toks == wide // (NZ // 2 * toks))).astype(bf16)

    down_recv = lax.all_to_all(down, ("z", "x"), 0, 0, tiled=True)
    down_recv = down_recv.reshape(NZ, NX, PIECE, width)

    h_own = hidden((part_a, part_b), gate, up)
    h_near = hidden((left_a, left_b, right_a, right_b), gate, up)
    early0 = jnp.concatenate([h_own, h_near])
    late0 = hidden((far_a, far_b), gate, up)
    early = {0: early0}
    late = {0: late0}
    for e in (1, 3, 2):
        early[e] = shift(early0, "x", NX, -e)
        late[e] = shift(late0, "x", NX, -e)
    pieces = (part_a, part_b, left_a, left_b, far_a, far_b, right_a, right_b)
    grad_sq = pick(sources, spread, pieces, cots, width)

    slot_table = slot_lookup(cluster, merged_slot)
    expert_ids = jnp.arange(EXPERTS, dtype=jnp.int32)
    member = first_expert + jnp.arange(NZ, dtype=jnp.int32)
    member_slot = jnp.sum(
        jnp.where(member[:, None] == expert_ids[None, :], slot_table[None, :], 0), axis=1
    )
    owner_core = (c + jnp.arange(NC, dtype=jnp.int32)) % NC
    owner_y = (y + jnp.arange(NY, dtype=jnp.int32)) % NY
    owner = owner_y[None, :] * NC + owner_core[:, None]
    slots = (owner[:, :, None] * OWN + jnp.arange(OWN, dtype=jnp.int32)).reshape(-1)
    same_slot = jnp.repeat(slots, PIECE)[:, None] == jnp.repeat(member_slot, PIECE)[None, :]
    q_row = jnp.arange(MERGED * PIECE, dtype=jnp.int32)[:, None] % PIECE
    q_col = jnp.arange(NZ * PIECE, dtype=jnp.int32)[None, :] % PIECE
    kron = (same_slot & (q_row == q_col)).astype(bf16)

    groups = []
    after = ()
    for half in HALVES:
        denom = fisher_half(half, early, late, grad_sq)
        denom_recv = lax.all_to_all(denom, ("z", "x"), 0, 0, tiled=True)
        mixed = mix(half, kron, denom_recv, down_recv, after)
        group, after = reduce_slots(*mixed)
        groups.append(group)
    return final(groups)


def solution(mesh):
    fine = Mesh(mesh.devices.reshape(NY, NC, NZ, NX), ("y", "c", "z", "x"))
    rows = P(("z", "x"), None)
    units = P(("y", "c", "z", "x"), None)

    return jax.shard_map(
        per_device,
        mesh=fine,
        in_specs=(rows, rows, rows, rows, units, units, units, P(), P()),
        out_specs=P(("y", "c"), None, ("z", "x"), None),
        check_vma=False,
    )
```

```python
import functools

import jax
import jax.numpy as jnp
from jax import lax
from jax.experimental import pallas as pl
from jax.experimental.pallas import tpu as pltpu
from jax.sharding import Mesh, PartitionSpec as P


F = 1024
EXPERTS = 64
MERGED = 24
CAP = 20
PRIOR = 0.1
NY, NC, NZ, NX = 4, 2, 8, 4
OWN = MERGED // (NY * NC)
ROWS = NZ * CAP
TALL = 24
STEPS = (0, 1, 7, 2, 6, 3, 5, 4)
PIECE = F // (NZ * NX * NX)
HALVES = ((0, 1), (3, 2))
ORDER = (0, 1, 3, 2)
HOPS = (1, 3, 0)
COLS = 7
INTERPRET = False


bf16 = jnp.bfloat16
f32 = jnp.float32


def shift(a, axis, size, step):
    return lax.ppermute(a, axis, [(i, (i + step) % size) for i in range(size)])


def slot_lookup(cluster, merged_slot):
    ids = jnp.arange(MERGED, dtype=jnp.int32)
    return jnp.sum(jnp.where(cluster[:, None] == ids[None, :], merged_slot[None, :], 0), axis=1)


def pack_kernel(here_ref, route_ref, weight_ref, tok_ref, *refs):
    outs, pick_ref, scale_ref = refs[:NZ], refs[NZ], refs[NZ + 1]
    toks, width = tok_ref.shape
    per = toks // (NY * NC)
    y, c, z = here_ref[0], here_ref[1], here_ref[2]
    first = (y * NC + c) * NZ
    routes = route_ref[...]
    weights = weight_ref[...]
    marks, scales = [], []
    for step in STEPS:
        match = routes == first + lax.rem(z + step, NZ)
        marks.append(jnp.sum(jnp.where(match, 1.0, 0.0), axis=0, keepdims=True))
        scales.append(jnp.sum(jnp.where(match, weights, 0.0), axis=0, keepdims=True))
    row = lax.broadcasted_iota(jnp.int32, (toks, toks), 0)
    col = lax.broadcasted_iota(jnp.int32, (toks, toks), 1)
    before = jnp.where(row < col, 1.0, 0.0).astype(bf16)
    marked = jnp.concatenate(marks, axis=0)
    places = jnp.dot(marked.astype(bf16), before, preferred_element_type=f32)
    place = lax.broadcasted_iota(jnp.int32, (TALL, toks), 0).astype(f32)
    for n in range(NZ):
        hit = (places[n : n + 1] == place) & (marks[n] > 0.0)
        pick_ref[n * TALL : (n + 1) * TALL, :] = jnp.where(hit, 1.0, 0.0)
        scale_ref[n * TALL : (n + 1) * TALL, :] = jnp.where(hit, scales[n], 0.0)
    pick = pick_ref[...].astype(bf16)
    step = width // COLS

    def body(k, carry):
        cols = pl.ds(pl.multiple_of(k * step, step), step)
        rows = jnp.dot(pick, tok_ref[:, cols], preferred_element_type=f32).astype(bf16)
        for n, out in enumerate(outs):
            out[:, cols] = rows[n * TALL : n * TALL + CAP]
        return carry

    lax.fori_loop(0, COLS, body, 0)
    ahead = lax.rem(y + col // (NC * per), NY)
    other = lax.rem(c + lax.rem(col // per, NC), NC)
    turned = (ahead * NC + other) * per + lax.rem(col, per)
    turn = jnp.where(row == turned, 1.0, 0.0).astype(bf16)
    scale = scale_ref[...]
    high = scale.astype(bf16)
    low = (scale - high.astype(f32)).astype(bf16)
    high = jnp.dot(high, turn, preferred_element_type=f32)
    low = jnp.dot(low, turn, preferred_element_type=f32)
    tail = jnp.concatenate([high, low], axis=1).astype(bf16)
    for n, out in enumerate(outs):
        out[:, width:] = tail[n * TALL : n * TALL + CAP]


def pack(here, routes, weights, tokens):
    toks, width = tokens.shape
    shape = jax.ShapeDtypeStruct((CAP, width + 2 * toks), bf16)
    return pl.pallas_call(
        pack_kernel,
        in_specs=[pl.BlockSpec(memory_space=pltpu.SMEM)] + [pl.BlockSpec(memory_space=pltpu.VMEM)] * 3,
        out_shape=[shape] * NZ,
        scratch_shapes=[pltpu.VMEM((NZ * TALL, toks), f32)] * 2,
        interpret=INTERPRET,
        name="pack",
    )(here, routes.T, weights.T, tokens)


def pick_kernel(here_ref, *refs):
    tails, cots, out_ref, tail_ref = refs[: 2 * NX], refs[2 * NX : -2], refs[-2], refs[-1]
    group = NZ // 2
    height = group * CAP
    per = cots[0].shape[2]
    tok = per * len(cots)
    row = lax.broadcasted_iota(jnp.int32, (height, group * tok), 0) // CAP
    col = lax.broadcasted_iota(jnp.int32, (height, group * tok), 1) // tok
    same = row == col
    lanes = tail_ref.shape[-1]
    lane = lax.broadcasted_iota(jnp.int32, (lanes, 2 * group * tok), 0)
    wide = lax.broadcasted_iota(jnp.int32, (lanes, 2 * group * tok), 1)
    match = (lane % tok == wide % tok) & (lane // tok == wide // (group * tok))
    spread = jnp.where(match, 1.0, 0.0).astype(bf16)
    z, x = here_ref[2], here_ref[3]
    for n, t in enumerate(tails):
        tail_ref[n] = t[...]

    def body(n, carry):
        half = n % 2
        xs = lax.rem(x + n // 2, NX)
        wide = jnp.dot(tail_ref[n], spread, preferred_element_type=f32)
        high = jnp.where(same, wide[:, : group * tok], 0.0).astype(bf16)
        low = jnp.where(same, wide[:, group * tok :], 0.0).astype(bf16)
        blocks = []
        for j in range(group):
            step = jnp.where(half == 0, STEPS[j], STEPS[group + j])
            zs = lax.rem(z + NZ - step, NZ)
            blocks += [cot[zs, xs].astype(f32) for cot in cots]
        cot = jnp.concatenate(blocks, axis=0).astype(bf16)
        val = jnp.dot(high, cot, preferred_element_type=f32)
        val = val + jnp.dot(low, cot, preferred_element_type=f32)
        val = val.astype(bf16).astype(f32)
        out_ref[n] = (val * val).astype(bf16)
        return carry

    lax.fori_loop(0, 2 * NX, body, 0)


def pick(here, pieces, cots, width):
    lanes = pieces[0].shape[1] - width
    height = pieces[0].shape[0]
    chunk = cots[0].shape[-1]
    tail = pl.BlockSpec((height, lanes), lambda i, src: (0, width // lanes))
    whole = lambda a: pl.BlockSpec(a.shape, lambda i, src: (0,) * a.ndim)
    return pl.pallas_call(
        pick_kernel,
        grid_spec=pltpu.PrefetchScalarGridSpec(
            num_scalar_prefetch=1,
            grid=(1,),
            in_specs=[tail] * len(pieces) + [whole(c) for c in cots],
            out_specs=pl.BlockSpec((2 * NX, ROWS // 2, chunk), lambda i, src: (0, 0, 0)),
            scratch_shapes=[pltpu.VMEM((2 * NX, height, lanes), bf16)],
        ),
        out_shape=jax.ShapeDtypeStruct((2 * NX, ROWS // 2, chunk), bf16),
        interpret=INTERPRET,
        name="pick",
    )(here, *pieces, *cots).reshape(NX, ROWS, chunk)


def hidden_kernel(*refs, pieces, known):
    blocks, gate_ref, up_ref = refs[:pieces], refs[pieces], refs[pieces + 1]
    outs, acc_ref = refs[pieces + 2 + known : -1], refs[-1]
    step = pl.program_id(0)
    rows = jnp.concatenate([b[...] for b in blocks], axis=0)
    units = gate_ref.shape[0]
    dims = (((1,), (1,)), ((), ()))
    g = lax.dot_general(rows, gate_ref[...], dims, preferred_element_type=f32)
    u = lax.dot_general(rows, up_ref[...], dims, preferred_element_type=f32)

    @pl.when(step == 0)
    def _():
        acc_ref[:, :units] = g
        acc_ref[:, units:] = u

    @pl.when(step > 0)
    def _():
        acc_ref[:, :units] += g
        acc_ref[:, units:] += u

    @pl.when(step == pl.num_programs(0) - 1)
    def _():
        gv = acc_ref[:, :units]
        h = gv / (1.0 + jnp.exp(-gv)) * acc_ref[:, units:]
        h = (h * h).astype(bf16)
        outs[0][...] = h
        if known:
            old = refs[pieces + 2]
            outs[1][: old.shape[0], :] = old[...]
            outs[1][old.shape[0] :, :] = h


def hidden(pieces, gate, up, *known):
    units, width = gate.shape
    step = width // NX
    total = sum(p.shape[0] for p in pieces)
    col = lambda k: (0, k)
    fixed = lambda k: (0, 0)
    heights = [total] + [total + k.shape[0] for k in known]
    return pl.pallas_call(
        functools.partial(hidden_kernel, pieces=len(pieces), known=len(known)),
        grid=(NX,),
        in_specs=[pl.BlockSpec((p.shape[0], step), col) for p in pieces]
        + [pl.BlockSpec((units, step), col)] * 2
        + [pl.BlockSpec(k.shape, fixed) for k in known],
        out_specs=[pl.BlockSpec((h, units), fixed) for h in heights],
        out_shape=[jax.ShapeDtypeStruct((h, units), bf16) for h in heights],
        scratch_shapes=[pltpu.VMEM((total, 2 * units), f32)],
        interpret=INTERPRET,
        name="hidden",
    )(*pieces, gate, up, *known)


def fisher_kernel(*refs, half, counts):
    g_ref, out_ref = refs[-2:]
    start = 0
    for j, count in enumerate(counts):
        e = half[j]
        parts = [r[...] for r in refs[start : start + count]]
        start += count
        h = jnp.concatenate(parts, axis=0) if count > 1 else parts[0]
        g = jnp.concatenate([g_ref[(e + d) % NX] for d in ORDER], axis=0)
        acc = lax.dot_general(h, g, (((0,), (0,)), ((), ())), preferred_element_type=f32)
        acc = acc + PRIOR
        out_ref[:, j * PIECE : (j + 1) * PIECE, :] = acc.reshape(-1, PIECE, acc.shape[1]).astype(bf16)


def fisher_half(half, parts, grad_sq):
    flat = [h for e in half for h in parts[e]]
    units = flat[0].shape[1] // 2
    chunk = grad_sq.shape[-1]
    return pl.pallas_call(
        functools.partial(fisher_kernel, half=half, counts=[len(parts[e]) for e in half]),
        grid=(2,),
        in_specs=[pl.BlockSpec((h.shape[0], units), lambda k: (0, k)) for h in flat]
        + [pl.BlockSpec(grad_sq.shape, lambda k: (0, 0, 0))],
        out_specs=pl.BlockSpec((NZ * NX // 2, 2 * PIECE, chunk), lambda k: (k, 0, 0)),
        out_shape=jax.ShapeDtypeStruct((NZ * NX, 2 * PIECE, chunk), bf16),
        interpret=INTERPRET,
        name="fisher",
    )(*flat, grad_sq)


def mix_kernel(kron_ref, den_ref, da_ref, db_ref, *refs):
    snd2_ref, snd_ref, own2_ref, own_ref, val_ref = refs[-5:]
    mix = kron_ref[...]
    block = OWN * PIECE
    for j, down_ref in enumerate((da_ref, db_ref)):
        den_all = den_ref[:, 0, j * PIECE : (j + 1) * PIECE, :].astype(f32)
        num_all = den_all * down_ref[:, 0].astype(f32)
        val_ref[2 * j] = num_all.reshape(NZ * PIECE, -1).astype(bf16)
        val_ref[2 * j + 1] = den_all.reshape(NZ * PIECE, -1).astype(bf16)

    def body(n, carry):
        arr = n % 2
        rows = pl.ds(pl.multiple_of(n // 2 * block, PIECE), block)
        res = jnp.dot(mix, val_ref[n], preferred_element_type=f32).astype(bf16)
        for core, (two, rest) in enumerate(((own2_ref, own_ref), (snd2_ref, snd_ref))):
            base = core * NY * block
            two[arr, rows, :] = res[base + 2 * block : base + 3 * block]
            for i, hop in enumerate(HOPS):
                rest[arr, i, rows, :] = res[base + hop * block : base + (hop + 1) * block]
        return carry

    lax.fori_loop(0, 4, body, 0)


def mix(half, kron, den, down, after):
    chunk = den.shape[-1]
    width = down.shape[-1]
    tall = 2 * OWN * PIECE
    two = jax.ShapeDtypeStruct((2, tall, width), bf16)
    rest = jax.ShapeDtypeStruct((2, len(HOPS), tall, width), bf16)
    two_spec = pl.BlockSpec((2, tall, chunk), lambda k: (0, 0, k))
    rest_spec = pl.BlockSpec((2, len(HOPS), tall, chunk), lambda k: (0, 0, 0, k))

    def down_spec(e):
        return pl.BlockSpec((NZ, 1, PIECE, chunk), lambda k: (0, lax.rem(k + e, NX), 0, k))

    return pl.pallas_call(
        mix_kernel,
        grid=(NX,),
        in_specs=[
            pl.BlockSpec(kron.shape, lambda k: (0, 0)),
            pl.BlockSpec((NZ, 1, 2 * PIECE, chunk), lambda k: (0, k, 0, 0)),
            down_spec(half[0]),
            down_spec(half[1]),
        ]
        + [pl.BlockSpec(memory_space=pl.ANY)] * len(after),
        out_specs=[two_spec, rest_spec, two_spec, rest_spec],
        out_shape=[two, rest, two, rest],
        scratch_shapes=[pltpu.VMEM((4, NZ * PIECE, chunk), bf16)],
        interpret=INTERPRET,
        name="mix",
    )(kron, den.reshape(NZ, NX, 2 * PIECE, chunk), down, down, *after)


def final_kernel(*refs):
    out_ref = refs[-1]
    block = OWN * PIECE
    k = pl.program_id(0)
    for n, half in enumerate(HALVES):
        own, oth, up_num, up_den, dn_num, dn_den = refs[6 * n : 6 * n + 6]
        tot = []
        for arr, up, dn in ((0, up_num, dn_num), (1, up_den, dn_den)):
            tot.append(
                own[arr, 0].astype(f32) + oth[arr, 0].astype(f32) + up[...].astype(f32) + dn[...].astype(f32)
            )
        res = (tot[0] / tot[1]).astype(bf16)
        for j, e in enumerate(half):
            s = lax.rem(k + e, NX)
            for m in range(OWN):
                out_ref[m, s] = res[j * block + m * PIECE : j * block + (m + 1) * PIECE]


def final(groups):
    tall, width = groups[0][2].shape
    chunk = width // NX
    flat = pl.BlockSpec((tall, chunk), lambda k: (0, k))
    rest = pl.BlockSpec((2, 1, tall, chunk), lambda k: (0, 2, 0, k))
    return pl.pallas_call(
        final_kernel,
        grid=(NX,),
        in_specs=[rest, rest, flat, flat, flat, flat] * 2,
        out_specs=pl.BlockSpec((OWN, NX, PIECE, chunk), lambda k: (0, 0, 0, k)),
        out_shape=jax.ShapeDtypeStruct((OWN, NX, PIECE, width), bf16),
        interpret=INTERPRET,
        name="final",
    )(*groups[0], *groups[1])


def sums_kernel(*refs, counts):
    outs = refs[-len(counts) :]
    step = outs[0].shape[1] // COLS

    def body(k, carry):
        cols = pl.ds(pl.multiple_of(k * step, step), step)
        start = 0
        for out, count in zip(outs, counts):
            total = refs[start][:, cols].astype(f32)
            for r in refs[start + 1 : start + count]:
                total = total + r[:, cols].astype(f32)
            out[:, cols] = total.astype(bf16)
            start += count
        return carry

    lax.fori_loop(0, COLS, body, 0)


def sums(*groups):
    specs, args = [], []
    for group in groups:
        for arr, lead in group:
            shape = (None,) * len(lead) + arr.shape[len(lead) :]
            specs.append(pl.BlockSpec(shape, lambda i, lead=lead: lead + (0, 0)))
            args.append(arr)
    shape = groups[0][0][0].shape[-2:]
    return pl.pallas_call(
        functools.partial(sums_kernel, counts=[len(g) for g in groups]),
        grid=(1,),
        in_specs=specs,
        out_specs=[pl.BlockSpec(shape, lambda i: (0, 0))] * len(groups),
        out_shape=[jax.ShapeDtypeStruct(shape, bf16)] * len(groups),
        interpret=INTERPRET,
        name="sums",
    )(*args)


def reduce_slots(snd2, snd, own2, own):
    oth2 = shift(snd2, "c", NC, 1)
    oth = shift(snd, "c", NC, 1)
    two_num, two_den = sums([(own2, (0,)), (oth2, (0,))], [(own2, (1,)), (oth2, (1,))])
    one_den, three_num = sums([(own, (1, 0)), (oth, (1, 0))], [(own, (0, 1)), (oth, (0, 1))])
    up1 = shift(two_num, "y", NY, 1)
    dn1 = shift(two_den, "y", NY, -1)
    up_den = shift(one_den, "y", NY, 1)
    dn_num = shift(three_num, "y", NY, -1)
    one_num, three_den = sums(
        [(own, (0, 0)), (oth, (0, 0)), (up1, ())], [(own, (1, 1)), (oth, (1, 1)), (dn1, ())]
    )
    up_num = shift(one_num, "y", NY, 1)
    dn_den = shift(three_den, "y", NY, -1)
    return (own, oth, up_num, up_den, dn_num, dn_den), (one_num, three_den)


def per_device(tokens, cotangent, routes, route_weights, gate, up, down, cluster, merged_slot):
    width = gate.shape[1]
    chunk = width // NX
    toks = tokens.shape[0]
    per = toks // (NY * NC)
    y, c = lax.axis_index("y"), lax.axis_index("c")
    z, x = lax.axis_index("z"), lax.axis_index("x")
    group = y * NC + c
    first_expert = group * NZ
    here = jnp.stack([y, c, z, x]).astype(jnp.int32)
    blocks = pack(here, routes, route_weights, tokens)
    got = [blocks[0]]
    for n, step in enumerate(STEPS[1:]):
        got.append(shift(blocks[n + 1], "z", NZ, step))
    part_a = jnp.concatenate(got[: NZ // 2])
    part_b = jnp.concatenate(got[NZ // 2 :])
    right_a = shift(part_a, "x", NX, 1)
    left_a = shift(part_a, "x", NX, -1)
    left_b = shift(part_b, "x", NX, -1)
    right_b = shift(part_b, "x", NX, 1)
    far_a = shift(right_a, "x", NX, 1)
    far_b = shift(left_b, "x", NX, -1)

    cot_own = lax.dynamic_slice_in_dim(cotangent, group * per, per, 0)
    cot_own = cot_own.reshape(per, NX, chunk).transpose(1, 0, 2)
    cot_send = jnp.broadcast_to(cot_own[None], (NZ, NX, per, chunk)).reshape(NZ * NX, per, chunk)
    cot0 = lax.all_to_all(cot_send, ("z", "x"), 0, 0, tiled=True)
    cot3 = shift(cot0, "y", NY, 1)
    cot1 = shift(cot0, "y", NY, -1)
    cot2 = shift(cot0, "y", NY, 2)
    cots = []
    for a in (cot0, cot1, cot2, cot3):
        b = shift(a, "c", NC, 1)
        cots += [a.reshape(NZ, NX, per, chunk), b.reshape(NZ, NX, per, chunk)]

    down_recv = lax.all_to_all(down, ("z", "x"), 0, 0, tiled=True)
    down_recv = down_recv.reshape(NZ, NX, PIECE, width)

    (main,) = hidden((part_a, part_b, left_a, left_b, right_a, right_b), gate, up)
    main1 = shift(main, "x", NX, -1)
    late, full = hidden((far_a, far_b), gate, up, main)
    late1 = shift(late, "x", NX, -1)
    full3 = shift(full, "x", NX, -3)
    full2 = shift(full, "x", NX, -2)
    parts = {0: (full,), 1: (main1, late1), 2: (full2,), 3: (full3,)}
    pieces = (part_a, part_b, left_a, left_b, far_a, far_b, right_a, right_b)
    grad_sq = pick(here, pieces, cots, width)

    slot_table = slot_lookup(cluster, merged_slot)
    expert_ids = jnp.arange(EXPERTS, dtype=jnp.int32)
    member = first_expert + jnp.arange(NZ, dtype=jnp.int32)
    member_slot = jnp.sum(
        jnp.where(member[:, None] == expert_ids[None, :], slot_table[None, :], 0), axis=1
    )
    owner_core = (c + jnp.arange(NC, dtype=jnp.int32)) % NC
    owner_y = (y + jnp.arange(NY, dtype=jnp.int32)) % NY
    owner = owner_y[None, :] * NC + owner_core[:, None]
    slots = (owner[:, :, None] * OWN + jnp.arange(OWN, dtype=jnp.int32)).reshape(-1)
    same_slot = jnp.repeat(slots, PIECE)[:, None] == jnp.repeat(member_slot, PIECE)[None, :]
    q_row = jnp.arange(MERGED * PIECE, dtype=jnp.int32)[:, None] % PIECE
    q_col = jnp.arange(NZ * PIECE, dtype=jnp.int32)[None, :] % PIECE
    kron = (same_slot & (q_row == q_col)).astype(bf16)

    groups = []
    after = ()
    for half in HALVES:
        denom = fisher_half(half, parts, grad_sq)
        denom_recv = lax.all_to_all(denom, ("z", "x"), 0, 0, tiled=True)
        mixed = mix(half, kron, denom_recv, down_recv, after)
        group, after = reduce_slots(*mixed)
        groups.append(group)
    return final(groups)


def solution(mesh):
    fine = Mesh(mesh.devices.reshape(NY, NC, NZ, NX), ("y", "c", "z", "x"))
    rows = P(("z", "x"), None)
    units = P(("y", "c", "z", "x"), None)

    return jax.shard_map(
        per_device,
        mesh=fine,
        in_specs=(rows, rows, rows, rows, units, units, units, P(), P()),
        out_specs=P(("y", "c"), None, ("z", "x"), None),
        check_vma=False,
    )
```

```python
import functools

import jax
import jax.numpy as jnp
from jax import lax
from jax.experimental import pallas as pl
from jax.experimental.pallas import tpu as pltpu
from jax.sharding import Mesh, PartitionSpec as P


F = 1024
EXPERTS = 64
MERGED = 24
CAP = 20
PRIOR = 0.1
NY, NC, NZ, NX = 4, 2, 8, 4
OWN = MERGED // (NY * NC)
ROWS = NZ * CAP
TALL = 24
STEPS = (0, 1, 7, 2, 6, 3, 5, 4)
PIECE = F // (NZ * NX * NX)
HALVES = ((0, 1), (3, 2))
ORDER = (0, 1, 3, 2)
HOPS = (1, 3, 0)
COLS = 7
INTERPRET = False


bf16 = jnp.bfloat16
f32 = jnp.float32


def shift(a, axis, size, step):
    return lax.ppermute(a, axis, [(i, (i + step) % size) for i in range(size)])


def slot_lookup(cluster, merged_slot):
    ids = jnp.arange(MERGED, dtype=jnp.int32)
    return jnp.sum(jnp.where(cluster[:, None] == ids[None, :], merged_slot[None, :], 0), axis=1)


def pack_kernel(here_ref, route_ref, weight_ref, tok_ref, *refs):
    outs, pick_ref, scale_ref = refs[:NZ], refs[NZ], refs[NZ + 1]
    toks, width = tok_ref.shape
    per = toks // (NY * NC)
    y, c, z = here_ref[0], here_ref[1], here_ref[2]
    first = (y * NC + c) * NZ
    routes = route_ref[...]
    weights = weight_ref[...]
    marks, scales = [], []
    for step in STEPS:
        match = routes == first + lax.rem(z + step, NZ)
        marks.append(jnp.sum(jnp.where(match, 1.0, 0.0), axis=0, keepdims=True))
        scales.append(jnp.sum(jnp.where(match, weights, 0.0), axis=0, keepdims=True))
    row = lax.broadcasted_iota(jnp.int32, (toks, toks), 0)
    col = lax.broadcasted_iota(jnp.int32, (toks, toks), 1)
    before = jnp.where(row < col, 1.0, 0.0).astype(bf16)
    marked = jnp.concatenate(marks, axis=0)
    places = jnp.dot(marked.astype(bf16), before, preferred_element_type=f32)
    place = lax.broadcasted_iota(jnp.int32, (TALL, toks), 0).astype(f32)
    for n in range(NZ):
        hit = (places[n : n + 1] == place) & (marks[n] > 0.0)
        pick_ref[n * TALL : (n + 1) * TALL, :] = jnp.where(hit, 1.0, 0.0)
        scale_ref[n * TALL : (n + 1) * TALL, :] = jnp.where(hit, scales[n], 0.0)
    pick = pick_ref[...].astype(bf16)
    step = width // COLS

    def body(k, carry):
        cols = pl.ds(pl.multiple_of(k * step, step), step)
        rows = jnp.dot(pick, tok_ref[:, cols], preferred_element_type=f32).astype(bf16)
        for n, out in enumerate(outs):
            out[:, cols] = rows[n * TALL : n * TALL + CAP]
        return carry

    lax.fori_loop(0, COLS, body, 0)
    ahead = lax.rem(y + col // (NC * per), NY)
    other = lax.rem(c + lax.rem(col // per, NC), NC)
    turned = (ahead * NC + other) * per + lax.rem(col, per)
    turn = jnp.where(row == turned, 1.0, 0.0).astype(bf16)
    scale = scale_ref[...]
    high = scale.astype(bf16)
    low = (scale - high.astype(f32)).astype(bf16)
    high = jnp.dot(high, turn, preferred_element_type=f32)
    low = jnp.dot(low, turn, preferred_element_type=f32)
    tail = jnp.concatenate([high, low], axis=1).astype(bf16)
    for n, out in enumerate(outs):
        out[:, width:] = tail[n * TALL : n * TALL + CAP]


def pack(here, routes, weights, tokens):
    toks, width = tokens.shape
    shape = jax.ShapeDtypeStruct((CAP, width + 2 * toks), bf16)
    return pl.pallas_call(
        pack_kernel,
        in_specs=[pl.BlockSpec(memory_space=pltpu.SMEM)] + [pl.BlockSpec(memory_space=pltpu.VMEM)] * 3,
        out_shape=[shape] * NZ,
        scratch_shapes=[pltpu.VMEM((NZ * TALL, toks), f32)] * 2,
        interpret=INTERPRET,
        name="pack",
    )(here, routes.T, weights.T, tokens)


def pick_kernel(here_ref, *refs, ahead):
    count = 2 * len(ahead)
    tails, cots, out_ref, tail_ref = refs[:count], refs[count:-2], refs[-2], refs[-1]
    group = NZ // 2
    height = group * CAP
    per = cots[0].shape[2]
    tok = per * len(cots)
    row = lax.broadcasted_iota(jnp.int32, (height, group * tok), 0) // CAP
    col = lax.broadcasted_iota(jnp.int32, (height, group * tok), 1) // tok
    same = row == col
    lanes = tail_ref.shape[-1]
    lane = lax.broadcasted_iota(jnp.int32, (lanes, 2 * group * tok), 0)
    wide = lax.broadcasted_iota(jnp.int32, (lanes, 2 * group * tok), 1)
    match = (lane % tok == wide % tok) & (lane // tok == wide // (group * tok))
    spread = jnp.where(match, 1.0, 0.0).astype(bf16)
    z, x = here_ref[2], here_ref[3]
    for n, t in enumerate(tails):
        tail_ref[n] = t[...]

    def body(n, carry):
        half = n % 2
        turn = ahead[0]
        for i in range(1, len(ahead)):
            turn = jnp.where(n // 2 == i, ahead[i], turn)
        xs = lax.rem(x + turn, NX)
        wide = jnp.dot(tail_ref[n], spread, preferred_element_type=f32)
        high = jnp.where(same, wide[:, : group * tok], 0.0).astype(bf16)
        low = jnp.where(same, wide[:, group * tok :], 0.0).astype(bf16)
        blocks = []
        for j in range(group):
            step = jnp.where(half == 0, STEPS[j], STEPS[group + j])
            zs = lax.rem(z + NZ - step, NZ)
            blocks += [cot[zs, xs].astype(f32) for cot in cots]
        cot = jnp.concatenate(blocks, axis=0).astype(bf16)
        val = jnp.dot(high, cot, preferred_element_type=f32)
        val = val + jnp.dot(low, cot, preferred_element_type=f32)
        val = val.astype(bf16).astype(f32)
        out_ref[n] = (val * val).astype(bf16)
        return carry

    lax.fori_loop(0, count, body, 0)


def pick(here, ahead, pieces, cots, width):
    lanes = pieces[0].shape[1] - width
    height = pieces[0].shape[0]
    chunk = cots[0].shape[-1]
    count = len(pieces)
    tail = pl.BlockSpec((height, lanes), lambda i, src: (0, width // lanes))
    whole = lambda a: pl.BlockSpec(a.shape, lambda i, src: (0,) * a.ndim)
    return pl.pallas_call(
        functools.partial(pick_kernel, ahead=ahead),
        grid_spec=pltpu.PrefetchScalarGridSpec(
            num_scalar_prefetch=1,
            grid=(1,),
            in_specs=[tail] * count + [whole(c) for c in cots],
            out_specs=pl.BlockSpec((count, ROWS // 2, chunk), lambda i, src: (0, 0, 0)),
            scratch_shapes=[pltpu.VMEM((count, height, lanes), bf16)],
        ),
        out_shape=jax.ShapeDtypeStruct((count, ROWS // 2, chunk), bf16),
        interpret=INTERPRET,
        name="pick",
    )(here, *pieces, *cots).reshape(count // 2, ROWS, chunk)


def hidden_kernel(*refs, pieces, known):
    blocks, gate_ref, up_ref = refs[:pieces], refs[pieces], refs[pieces + 1]
    outs, acc_ref = refs[pieces + 2 + known : -1], refs[-1]
    step = pl.program_id(0)
    rows = jnp.concatenate([b[...] for b in blocks], axis=0)
    units = gate_ref.shape[0]
    dims = (((1,), (1,)), ((), ()))
    g = lax.dot_general(rows, gate_ref[...], dims, preferred_element_type=f32)
    u = lax.dot_general(rows, up_ref[...], dims, preferred_element_type=f32)

    @pl.when(step == 0)
    def _():
        acc_ref[:, :units] = g
        acc_ref[:, units:] = u

    @pl.when(step > 0)
    def _():
        acc_ref[:, :units] += g
        acc_ref[:, units:] += u

    @pl.when(step == pl.num_programs(0) - 1)
    def _():
        gv = acc_ref[:, :units]
        h = gv / (1.0 + jnp.exp(-gv)) * acc_ref[:, units:]
        h = (h * h).astype(bf16)
        outs[0][...] = h
        if known:
            old = refs[pieces + 2]
            outs[1][: old.shape[0], :] = old[...]
            outs[1][old.shape[0] :, :] = h


def hidden(count, pieces, gate, up, *known):
    units, width = gate.shape
    step = width // count
    total = sum(p.shape[0] for p in pieces)
    col = lambda k: (0, k)
    fixed = lambda k: (0, 0)
    heights = [total] + [total + k.shape[0] for k in known]
    return pl.pallas_call(
        functools.partial(hidden_kernel, pieces=len(pieces), known=len(known)),
        grid=(count,),
        in_specs=[pl.BlockSpec((p.shape[0], step), col) for p in pieces]
        + [pl.BlockSpec((units, step), col)] * 2
        + [pl.BlockSpec(k.shape, fixed) for k in known],
        out_specs=[pl.BlockSpec((h, units), fixed) for h in heights],
        out_shape=[jax.ShapeDtypeStruct((h, units), bf16) for h in heights],
        scratch_shapes=[pltpu.VMEM((total, 2 * units), f32)],
        interpret=INTERPRET,
        name="hidden",
    )(*pieces, gate, up, *known)


def fisher_kernel(*refs, half, counts):
    near_ref, far_ref, out_ref = refs[-3:]
    grads = {r: near_ref.at[i] for i, r in enumerate(ORDER[:3])}
    grads[ORDER[3]] = far_ref.at[0]
    start = 0
    for j, count in enumerate(counts):
        e = half[j]
        parts = [r[...] for r in refs[start : start + count]]
        start += count
        h = jnp.concatenate(parts, axis=0) if count > 1 else parts[0]
        g = jnp.concatenate([grads[(e + d) % NX][...] for d in ORDER], axis=0)
        acc = lax.dot_general(h, g, (((0,), (0,)), ((), ())), preferred_element_type=f32)
        acc = acc + PRIOR
        out_ref[:, j * PIECE : (j + 1) * PIECE, :] = acc.reshape(-1, PIECE, acc.shape[1]).astype(bf16)


def fisher_half(half, parts, near, far):
    flat = [h for e in half for h in parts[e]]
    units = flat[0].shape[1] // 2
    chunk = near.shape[-1]
    return pl.pallas_call(
        functools.partial(fisher_kernel, half=half, counts=[len(parts[e]) for e in half]),
        grid=(2,),
        in_specs=[pl.BlockSpec((h.shape[0], units), lambda k: (0, k)) for h in flat]
        + [pl.BlockSpec(a.shape, lambda k: (0, 0, 0)) for a in (near, far)],
        out_specs=pl.BlockSpec((NZ * NX // 2, 2 * PIECE, chunk), lambda k: (k, 0, 0)),
        out_shape=jax.ShapeDtypeStruct((NZ * NX, 2 * PIECE, chunk), bf16),
        interpret=INTERPRET,
        name="fisher",
    )(*flat, near, far)


def mix_kernel(spot_ref, den_ref, da_ref, db_ref, *refs):
    two, rest, val_ref, acc_ref = refs[-6:-4], refs[-4:-2], refs[-2], refs[-1]
    for j, down_ref in enumerate((da_ref, db_ref)):
        den = den_ref[:, 0, j * PIECE : (j + 1) * PIECE, :].astype(f32)
        val_ref[2 * j + 1] = den.astype(f32)
        val_ref[2 * j] = (den * down_ref[:, 0].astype(f32)).astype(bf16).astype(f32)

    def body(n, carry):
        arr = n % 2
        rows = pl.ds(pl.multiple_of(n // 2 * OWN * PIECE, PIECE), OWN * PIECE)
        acc_ref[...] = jnp.zeros(acc_ref.shape, f32)
        for i in range(NZ):
            acc_ref[spot_ref[i]] += val_ref[n, i]
        for core in range(NC):
            for hop in range(NY):
                start = (core * NY + hop) * OWN
                res = acc_ref[start : start + OWN]
                res = res.reshape(OWN * PIECE, res.shape[-1]).astype(bf16)
                if hop == 2:
                    two[core][arr, rows, :] = res
                else:
                    rest[core][arr, HOPS.index(hop), rows, :] = res
        return carry

    lax.fori_loop(0, 4, body, 0)


def mix(half, spots, den, down, after):
    chunk = den.shape[-1]
    width = down.shape[-1]
    tall = 2 * OWN * PIECE
    two = jax.ShapeDtypeStruct((2, tall, width), bf16)
    rest = jax.ShapeDtypeStruct((2, len(HOPS), tall, width), bf16)
    two_spec = pl.BlockSpec((2, tall, chunk), lambda k: (0, 0, k))
    rest_spec = pl.BlockSpec((2, len(HOPS), tall, chunk), lambda k: (0, 0, 0, k))

    def down_spec(e):
        return pl.BlockSpec((NZ, 1, PIECE, chunk), lambda k: (0, lax.rem(k + e, NX), 0, k))

    return pl.pallas_call(
        mix_kernel,
        grid=(NX,),
        in_specs=[
            pl.BlockSpec(memory_space=pltpu.SMEM),
            pl.BlockSpec((NZ, 1, 2 * PIECE, chunk), lambda k: (0, k, 0, 0)),
            down_spec(half[0]),
            down_spec(half[1]),
        ]
        + [pl.BlockSpec(memory_space=pl.ANY)] * len(after),
        out_specs=[two_spec, two_spec, rest_spec, rest_spec],
        out_shape=[two, two, rest, rest],
        scratch_shapes=[
            pltpu.VMEM((4, NZ, PIECE, chunk), f32),
            pltpu.VMEM((MERGED, PIECE, chunk), f32),
        ],
        interpret=INTERPRET,
        name="mix",
    )(spots, den.reshape(NZ, NX, 2 * PIECE, chunk), down, down, *after)


def final_kernel(*refs):
    own, oth, up_num, up_den, dn_num, dn_den = refs[:6]
    out_ref = refs[-1]
    tot = []
    for arr, up, dn in ((0, up_num, dn_num), (1, up_den, dn_den)):
        tot.append(
            own[arr, 0].astype(f32) + oth[arr, 0].astype(f32) + up[...].astype(f32) + dn[...].astype(f32)
        )
    res = (tot[0] / tot[1]).astype(bf16)
    for m in range(OWN):
        out_ref[m, 0] = res[m * PIECE : (m + 1) * PIECE]


def final(half, group, *before):
    _, width = group[2].shape
    chunk = width // NX
    block = OWN * PIECE
    flat = pl.BlockSpec((block, chunk), lambda k, j: (j, k))
    rest = pl.BlockSpec((2, 1, block, chunk), lambda k, j: (0, 2, j, k))
    first, gap = half[0], half[1] - half[0]
    return pl.pallas_call(
        final_kernel,
        grid=(NX, 2),
        in_specs=[rest, rest, flat, flat, flat, flat] + [pl.BlockSpec(memory_space=pl.ANY)] * len(before),
        out_specs=pl.BlockSpec(
            (OWN, 1, PIECE, chunk), lambda k, j: (0, lax.rem(k + first + gap * j, NX), 0, k)
        ),
        out_shape=jax.ShapeDtypeStruct((OWN, NX, PIECE, width), bf16),
        input_output_aliases={6: 0} if before else {},
        interpret=INTERPRET,
        name="final",
    )(*group, *before)


def sums(*groups):
    outs = []
    for group in groups:
        total = 0.0
        for arr, lead in group:
            total = total + arr[lead].astype(f32)
        outs.append(total.astype(bf16))
    return outs


def reduce_slots(snd2, snd, own2, own):
    oth2 = shift(snd2, "c", NC, 1)
    oth = shift(snd, "c", NC, 1)
    two_num, two_den = sums([(own2, (0,)), (oth2, (0,))], [(own2, (1,)), (oth2, (1,))])
    one_den, three_num = sums([(own, (1, 0)), (oth, (1, 0))], [(own, (0, 1)), (oth, (0, 1))])
    up1 = shift(two_num, "y", NY, 1)
    dn1 = shift(two_den, "y", NY, -1)
    up_den = shift(one_den, "y", NY, 1)
    dn_num = shift(three_num, "y", NY, -1)
    one_num, three_den = sums(
        [(own, (0, 0)), (oth, (0, 0)), (up1, ())], [(own, (1, 1)), (oth, (1, 1)), (dn1, ())]
    )
    up_num = shift(one_num, "y", NY, 1)
    dn_den = shift(three_den, "y", NY, -1)
    return (own, oth, up_num, up_den, dn_num, dn_den), (one_num, three_den)


def per_device(tokens, cotangent, routes, route_weights, gate, up, down, cluster, merged_slot):
    width = gate.shape[1]
    chunk = width // NX
    toks = tokens.shape[0]
    per = toks // (NY * NC)
    y, c = lax.axis_index("y"), lax.axis_index("c")
    z, x = lax.axis_index("z"), lax.axis_index("x")
    group = y * NC + c
    first_expert = group * NZ
    here = jnp.stack([y, c, z, x]).astype(jnp.int32)
    blocks = pack(here, routes, route_weights, tokens)
    got = [blocks[0]]
    for n, step in enumerate(STEPS[1:]):
        got.append(shift(blocks[n + 1], "z", NZ, step))
    part_a = jnp.concatenate(got[: NZ // 2])
    part_b = jnp.concatenate(got[NZ // 2 :])
    right_a = shift(part_a, "x", NX, 1)
    left_a = shift(part_a, "x", NX, -1)
    left_b = shift(part_b, "x", NX, -1)
    right_b = shift(part_b, "x", NX, 1)
    far_a = shift(right_a, "x", NX, 1)
    far_b = shift(left_b, "x", NX, -1)

    cot_own = lax.dynamic_slice_in_dim(cotangent, group * per, per, 0)
    cot_own = cot_own.reshape(per, NX, chunk).transpose(1, 0, 2)
    cot_send = jnp.broadcast_to(cot_own[None], (NZ, NX, per, chunk)).reshape(NZ * NX, per, chunk)
    cot0 = lax.all_to_all(cot_send, ("z", "x"), 0, 0, tiled=True)
    cot3 = shift(cot0, "y", NY, 1)
    cot1 = shift(cot0, "y", NY, -1)
    cot2 = shift(cot0, "y", NY, 2)
    cots = []
    for a in (cot0, cot1, cot2, cot3):
        b = shift(a, "c", NC, 1)
        cots += [a.reshape(NZ, NX, per, chunk), b.reshape(NZ, NX, per, chunk)]

    down_recv = lax.all_to_all(down, ("z", "x"), 0, 0, tiled=True)
    down_recv = down_recv.reshape(NZ, NX, PIECE, width)

    (main,) = hidden(COLS, (part_a, part_b, left_a, left_b, right_a, right_b), gate, up)
    main1 = shift(main, "x", NX, -1)
    late, full = hidden(NX, (far_a, far_b), gate, up, main)
    late1 = shift(late, "x", NX, -1)
    full3 = shift(full, "x", NX, -3)
    full2 = shift(full, "x", NX, -2)
    parts = {0: (full,), 1: (main1, late1), 2: (full2,), 3: (full3,)}
    near = (part_a, part_b, left_a, left_b, right_a, right_b)
    grad_near = pick(here, ORDER[:3], near, cots, width)
    grad_far = pick(here, ORDER[3:], (far_a, far_b), cots, width)

    slot_table = slot_lookup(cluster, merged_slot)
    expert_ids = jnp.arange(EXPERTS, dtype=jnp.int32)
    member = first_expert + jnp.arange(NZ, dtype=jnp.int32)
    member_slot = jnp.sum(
        jnp.where(member[:, None] == expert_ids[None, :], slot_table[None, :], 0), axis=1
    )
    owner, row = member_slot // OWN, member_slot % OWN
    core, hop = (owner % NC - c) % NC, (owner // NC - y) % NY
    spots = (core * NY + hop) * OWN + row

    groups = []
    after = ()
    for half in HALVES:
        denom = fisher_half(half, parts, grad_near, grad_far)
        denom_recv = lax.all_to_all(denom, ("z", "x"), 0, 0, tiled=True)
        mixed = mix(half, spots, denom_recv, down_recv, after)
        own2, snd2, own, snd = mixed
        group, after = reduce_slots(snd2, snd, own2, own)
        groups.append(group)
    first = final(HALVES[0], groups[0])
    return final(HALVES[1], groups[1], first)


def solution(mesh):
    fine = Mesh(mesh.devices.reshape(NY, NC, NZ, NX), ("y", "c", "z", "x"))
    rows = P(("z", "x"), None)
    units = P(("y", "c", "z", "x"), None)

    return jax.shard_map(
        per_device,
        mesh=fine,
        in_specs=(rows, rows, rows, rows, units, units, units, P(), P()),
        out_specs=P(("y", "c"), None, ("z", "x"), None),
        check_vma=False,
    )
```

```python
import functools

import jax
import jax.numpy as jnp
from jax import lax
from jax.experimental import pallas as pl
from jax.experimental.pallas import tpu as pltpu
from jax.sharding import Mesh, PartitionSpec as P


F = 1024
EXPERTS = 64
MERGED = 24
CAP = 20
PRIOR = 0.1
NY, NC, NZ, NX = 4, 2, 8, 4
OWN = MERGED // (NY * NC)
ROWS = NZ * CAP
TALL = 24
STEPS = (0, 1, 7, 2, 6, 3, 5, 4)
PIECE = F // (NZ * NX * NX)
HALVES = ((0, 1), (3, 2))
ORDER = (0, 1, 3, 2)
HOPS = (1, 3, 0)
COLS = 7
INTERPRET = False


bf16 = jnp.bfloat16
f32 = jnp.float32


def shift(a, axis, size, step):
    return lax.ppermute(a, axis, [(i, (i + step) % size) for i in range(size)])


def slot_lookup(cluster, merged_slot):
    ids = jnp.arange(MERGED, dtype=jnp.int32)
    return jnp.sum(jnp.where(cluster[:, None] == ids[None, :], merged_slot[None, :], 0), axis=1)


def pack_kernel(here_ref, route_ref, weight_ref, tok_ref, *refs):
    outs, pick_ref, scale_ref = refs[:NZ], refs[NZ], refs[NZ + 1]
    toks, width = tok_ref.shape
    per = toks // (NY * NC)
    y, c, z = here_ref[0], here_ref[1], here_ref[2]
    first = (y * NC + c) * NZ
    routes = route_ref[...]
    weights = weight_ref[...]
    marks, scales = [], []
    for step in STEPS:
        match = routes == first + lax.rem(z + step, NZ)
        marks.append(jnp.sum(jnp.where(match, 1.0, 0.0), axis=0, keepdims=True))
        scales.append(jnp.sum(jnp.where(match, weights, 0.0), axis=0, keepdims=True))
    row = lax.broadcasted_iota(jnp.int32, (toks, toks), 0)
    col = lax.broadcasted_iota(jnp.int32, (toks, toks), 1)
    before = jnp.where(row < col, 1.0, 0.0).astype(bf16)
    marked = jnp.concatenate(marks, axis=0)
    places = jnp.dot(marked.astype(bf16), before, preferred_element_type=f32)
    place = lax.broadcasted_iota(jnp.int32, (TALL, toks), 0).astype(f32)
    for n in range(NZ):
        hit = (places[n : n + 1] == place) & (marks[n] > 0.0)
        pick_ref[n * TALL : (n + 1) * TALL, :] = jnp.where(hit, 1.0, 0.0)
        scale_ref[n * TALL : (n + 1) * TALL, :] = jnp.where(hit, scales[n], 0.0)
    pick = pick_ref[...].astype(bf16)
    step = width // COLS

    def body(k, carry):
        cols = pl.ds(pl.multiple_of(k * step, step), step)
        rows = jnp.dot(pick, tok_ref[:, cols], preferred_element_type=f32).astype(bf16)
        for n, out in enumerate(outs):
            out[:, cols] = rows[n * TALL : n * TALL + CAP]
        return carry

    lax.fori_loop(0, COLS, body, 0)
    ahead = lax.rem(y + col // (NC * per), NY)
    other = lax.rem(c + lax.rem(col // per, NC), NC)
    turned = (ahead * NC + other) * per + lax.rem(col, per)
    turn = jnp.where(row == turned, 1.0, 0.0).astype(bf16)
    scale = scale_ref[...]
    high = scale.astype(bf16)
    low = (scale - high.astype(f32)).astype(bf16)
    high = jnp.dot(high, turn, preferred_element_type=f32)
    low = jnp.dot(low, turn, preferred_element_type=f32)
    tail = jnp.concatenate([high, low], axis=1).astype(bf16)
    for n, out in enumerate(outs):
        out[:, width:] = tail[n * TALL : n * TALL + CAP]


def pack(here, routes, weights, tokens):
    toks, width = tokens.shape
    shape = jax.ShapeDtypeStruct((CAP, width + 2 * toks), bf16)
    return pl.pallas_call(
        pack_kernel,
        in_specs=[pl.BlockSpec(memory_space=pltpu.SMEM)] + [pl.BlockSpec(memory_space=pltpu.VMEM)] * 3,
        out_shape=[shape] * NZ,
        scratch_shapes=[pltpu.VMEM((NZ * TALL, toks), f32)] * 2,
        interpret=INTERPRET,
        name="pack",
    )(here, routes.T, weights.T, tokens)


def pick_kernel(here_ref, *refs, ahead):
    count = 2 * len(ahead)
    tails, cots, out_ref, tail_ref = refs[:count], refs[count:-2], refs[-2], refs[-1]
    group = NZ // 2
    height = group * CAP
    per = cots[0].shape[2]
    tok = per * len(cots)
    row = lax.broadcasted_iota(jnp.int32, (height, group * tok), 0) // CAP
    col = lax.broadcasted_iota(jnp.int32, (height, group * tok), 1) // tok
    same = row == col
    lanes = tail_ref.shape[-1]
    lane = lax.broadcasted_iota(jnp.int32, (lanes, 2 * group * tok), 0)
    wide = lax.broadcasted_iota(jnp.int32, (lanes, 2 * group * tok), 1)
    match = (lane % tok == wide % tok) & (lane // tok == wide // (group * tok))
    spread = jnp.where(match, 1.0, 0.0).astype(bf16)
    z, x = here_ref[2], here_ref[3]
    for n, t in enumerate(tails):
        tail_ref[n] = t[...]

    def body(n, carry):
        half = n % 2
        turn = ahead[0]
        for i in range(1, len(ahead)):
            turn = jnp.where(n // 2 == i, ahead[i], turn)
        xs = lax.rem(x + turn, NX)
        wide = jnp.dot(tail_ref[n], spread, preferred_element_type=f32)
        high = jnp.where(same, wide[:, : group * tok], 0.0).astype(bf16)
        low = jnp.where(same, wide[:, group * tok :], 0.0).astype(bf16)
        blocks = []
        for j in range(group):
            step = jnp.where(half == 0, STEPS[j], STEPS[group + j])
            zs = lax.rem(z + NZ - step, NZ)
            blocks += [cot[zs, xs if cot.shape[1] > 1 else 0].astype(f32) for cot in cots]
        cot = jnp.concatenate(blocks, axis=0).astype(bf16)
        val = jnp.dot(high, cot, preferred_element_type=f32)
        val = val + jnp.dot(low, cot, preferred_element_type=f32)
        val = val.astype(bf16).astype(f32)
        out_ref[n] = (val * val).astype(bf16)
        return carry

    lax.fori_loop(0, count, body, 0)


def pick(here, ahead, pieces, cots, width):
    lanes = pieces[0].shape[1] - width
    height = pieces[0].shape[0]
    chunk = cots[0].shape[-1]
    count = len(pieces)
    tail = pl.BlockSpec((height, lanes), lambda i, src: (0, width // lanes))
    if len(ahead) > 1:
        part = lambda a: pl.BlockSpec(a.shape, lambda i, src: (0, 0, 0, 0))
    else:
        part = lambda a: pl.BlockSpec(
            (NZ, 1) + a.shape[2:], lambda i, src: (0, lax.rem(src[3] + ahead[0], NX), 0, 0)
        )
    return pl.pallas_call(
        functools.partial(pick_kernel, ahead=ahead),
        grid_spec=pltpu.PrefetchScalarGridSpec(
            num_scalar_prefetch=1,
            grid=(1,),
            in_specs=[tail] * count + [part(c) for c in cots],
            out_specs=pl.BlockSpec((count, ROWS // 2, chunk), lambda i, src: (0, 0, 0)),
            scratch_shapes=[pltpu.VMEM((count, height, lanes), bf16)],
        ),
        out_shape=jax.ShapeDtypeStruct((count, ROWS // 2, chunk), bf16),
        interpret=INTERPRET,
        name="pick",
    )(here, *pieces, *cots).reshape(count // 2, ROWS, chunk)


def hidden_kernel(*refs, pieces, known):
    blocks, gate_ref, up_ref = refs[:pieces], refs[pieces], refs[pieces + 1]
    outs, acc_ref = refs[pieces + 2 + known : -1], refs[-1]
    step = pl.program_id(0)
    rows = jnp.concatenate([b[...] for b in blocks], axis=0)
    units = gate_ref.shape[0]
    dims = (((1,), (1,)), ((), ()))
    g = lax.dot_general(rows, gate_ref[...], dims, preferred_element_type=f32)
    u = lax.dot_general(rows, up_ref[...], dims, preferred_element_type=f32)

    @pl.when(step == 0)
    def _():
        acc_ref[:, :units] = g
        acc_ref[:, units:] = u

    @pl.when(step > 0)
    def _():
        acc_ref[:, :units] += g
        acc_ref[:, units:] += u

    @pl.when(step == pl.num_programs(0) - 1)
    def _():
        gv = acc_ref[:, :units]
        h = gv / (1.0 + jnp.exp(-gv)) * acc_ref[:, units:]
        h = (h * h).astype(bf16)
        outs[0][...] = h
        if known:
            old = refs[pieces + 2]
            outs[1][: old.shape[0], :] = old[...]
            outs[1][old.shape[0] :, :] = h


def hidden(count, pieces, gate, up, *known):
    units, width = gate.shape
    step = width // count
    total = sum(p.shape[0] for p in pieces)
    col = lambda k: (0, k)
    fixed = lambda k: (0, 0)
    heights = [total] + [total + k.shape[0] for k in known]
    return pl.pallas_call(
        functools.partial(hidden_kernel, pieces=len(pieces), known=len(known)),
        grid=(count,),
        in_specs=[pl.BlockSpec((p.shape[0], step), col) for p in pieces]
        + [pl.BlockSpec((units, step), col)] * 2
        + [pl.BlockSpec(k.shape, fixed) for k in known],
        out_specs=[pl.BlockSpec((h, units), fixed) for h in heights],
        out_shape=[jax.ShapeDtypeStruct((h, units), bf16) for h in heights],
        scratch_shapes=[pltpu.VMEM((total, 2 * units), f32)],
        interpret=INTERPRET,
        name="hidden",
    )(*pieces, gate, up, *known)


def fisher_kernel(*refs, half, counts):
    near_ref, far_ref, out_ref = refs[-3:]
    grads = {r: near_ref.at[i] for i, r in enumerate(ORDER[:3])}
    grads[ORDER[3]] = far_ref.at[0]
    start = 0
    for j, count in enumerate(counts):
        e = half[j]
        parts = [r[...] for r in refs[start : start + count]]
        start += count
        h = jnp.concatenate(parts, axis=0) if count > 1 else parts[0]
        g = jnp.concatenate([grads[(e + d) % NX][...] for d in ORDER], axis=0)
        acc = lax.dot_general(h, g, (((0,), (0,)), ((), ())), preferred_element_type=f32)
        acc = acc + PRIOR
        out_ref[:, j * PIECE : (j + 1) * PIECE, :] = acc.reshape(-1, PIECE, acc.shape[1]).astype(bf16)


def fisher_half(half, parts, near, far):
    flat = [h for e in half for h in parts[e]]
    units = flat[0].shape[1] // 2
    chunk = near.shape[-1]
    return pl.pallas_call(
        functools.partial(fisher_kernel, half=half, counts=[len(parts[e]) for e in half]),
        grid=(2,),
        in_specs=[pl.BlockSpec((h.shape[0], units), lambda k: (0, k)) for h in flat]
        + [pl.BlockSpec(a.shape, lambda k: (0, 0, 0)) for a in (near, far)],
        out_specs=pl.BlockSpec((NZ * NX // 2, 2 * PIECE, chunk), lambda k: (k, 0, 0)),
        out_shape=jax.ShapeDtypeStruct((NZ * NX, 2 * PIECE, chunk), bf16),
        interpret=INTERPRET,
        name="fisher",
    )(*flat, near, far)


def mix_kernel(spot_ref, den_ref, da_ref, db_ref, *refs):
    two, rest, val_ref, acc_ref = refs[-6:-4], refs[-4:-2], refs[-2], refs[-1]
    den = den_ref[:, 0]
    down = jnp.concatenate([da_ref[:, 0].astype(f32), db_ref[:, 0].astype(f32)], axis=1)
    val_ref[0] = (den.astype(f32) * down).astype(bf16)
    val_ref[1] = den

    def body(arr, carry):
        acc_ref[...] = jnp.zeros(acc_ref.shape, bf16)
        for i in range(NZ):
            acc_ref[spot_ref[i]] += val_ref[arr, i]
        for core in range(NC):
            for hop in range(NY):
                start = (core * NY + hop) * OWN
                res = acc_ref[start : start + OWN]
                res = res.reshape(OWN * 2 * PIECE, res.shape[-1])
                if hop == 2:
                    two[core][arr] = res
                else:
                    rest[core][arr, HOPS.index(hop)] = res
        return carry

    lax.fori_loop(0, 2, body, 0)


def mix(half, spots, den, down):
    chunk = den.shape[-1]
    width = down.shape[-1]
    tall = 2 * OWN * PIECE
    two = jax.ShapeDtypeStruct((2, tall, width), bf16)
    rest = jax.ShapeDtypeStruct((2, len(HOPS), tall, width), bf16)
    two_spec = pl.BlockSpec((2, tall, chunk), lambda k: (0, 0, k))
    rest_spec = pl.BlockSpec((2, len(HOPS), tall, chunk), lambda k: (0, 0, 0, k))

    def down_spec(e):
        return pl.BlockSpec((NZ, 1, PIECE, chunk), lambda k: (0, lax.rem(k + e, NX), 0, k))

    return pl.pallas_call(
        mix_kernel,
        grid=(NX,),
        in_specs=[
            pl.BlockSpec(memory_space=pltpu.SMEM),
            pl.BlockSpec((NZ, 1, 2 * PIECE, chunk), lambda k: (0, k, 0, 0)),
            down_spec(half[0]),
            down_spec(half[1]),
        ],
        out_specs=[two_spec, two_spec, rest_spec, rest_spec],
        out_shape=[two, two, rest, rest],
        scratch_shapes=[
            pltpu.VMEM((2, NZ, 2 * PIECE, chunk), bf16),
            pltpu.VMEM((MERGED, 2 * PIECE, chunk), bf16),
        ],
        interpret=INTERPRET,
        name="mix",
    )(spots, den.reshape(NZ, NX, 2 * PIECE, chunk), down, down)


def ratio(group):
    own, oth, up_num, up_den, dn_num, dn_den = group
    num = own[0, 2].astype(f32) + oth[0, 2].astype(f32) + up_num.astype(f32) + dn_num.astype(f32)
    den = own[1, 2].astype(f32) + oth[1, 2].astype(f32) + up_den.astype(f32) + dn_den.astype(f32)
    return (num / den).astype(bf16)


def final_kernel(first_ref, own, oth, up_num, up_den, dn_num, dn_den, out_ref):
    k = pl.program_id(0)
    tot = []
    for arr, up, dn in ((0, up_num, dn_num), (1, up_den, dn_den)):
        tot.append(
            own[arr, 0].astype(f32) + oth[arr, 0].astype(f32) + up[...].astype(f32) + dn[...].astype(f32)
        )
    second = (tot[0] / tot[1]).astype(bf16)
    for half, res in zip(HALVES, (first_ref[...], second)):
        for j, e in enumerate(half):
            s = lax.rem(k + e, NX)
            for m in range(OWN):
                start = (2 * m + j) * PIECE
                out_ref[m, s] = res[start : start + PIECE]


def final(first, group):
    tall, width = first.shape
    chunk = width // NX
    flat = pl.BlockSpec((tall, chunk), lambda k: (0, k))
    rest = pl.BlockSpec((2, 1, tall, chunk), lambda k: (0, 2, 0, k))
    return pl.pallas_call(
        final_kernel,
        grid=(NX,),
        in_specs=[flat, rest, rest, flat, flat, flat, flat],
        out_specs=pl.BlockSpec((OWN, NX, PIECE, chunk), lambda k: (0, 0, 0, k)),
        out_shape=jax.ShapeDtypeStruct((OWN, NX, PIECE, width), bf16),
        interpret=INTERPRET,
        name="final",
    )(first, *group)


def sums(*groups):
    outs = []
    for group in groups:
        total = 0.0
        for arr, lead in group:
            total = total + arr[lead].astype(f32)
        outs.append(total.astype(bf16))
    return outs


def reduce_slots(snd2, snd, own2, own):
    oth2 = shift(snd2, "c", NC, 1)
    oth = shift(snd, "c", NC, 1)
    two_num, two_den = sums([(own2, (0,)), (oth2, (0,))], [(own2, (1,)), (oth2, (1,))])
    one_den, three_num = sums([(own, (1, 0)), (oth, (1, 0))], [(own, (0, 1)), (oth, (0, 1))])
    up1 = shift(two_num, "y", NY, 1)
    dn1 = shift(two_den, "y", NY, -1)
    up_den = shift(one_den, "y", NY, 1)
    dn_num = shift(three_num, "y", NY, -1)
    one_num, three_den = sums(
        [(own, (0, 0)), (oth, (0, 0)), (up1, ())], [(own, (1, 1)), (oth, (1, 1)), (dn1, ())]
    )
    up_num = shift(one_num, "y", NY, 1)
    dn_den = shift(three_den, "y", NY, -1)
    return own, oth, up_num, up_den, dn_num, dn_den


def per_device(tokens, cotangent, routes, route_weights, gate, up, down, cluster, merged_slot):
    width = gate.shape[1]
    chunk = width // NX
    toks = tokens.shape[0]
    per = toks // (NY * NC)
    y, c = lax.axis_index("y"), lax.axis_index("c")
    z, x = lax.axis_index("z"), lax.axis_index("x")
    group = y * NC + c
    first_expert = group * NZ
    here = jnp.stack([y, c, z, x]).astype(jnp.int32)
    blocks = pack(here, routes, route_weights, tokens)
    got = [blocks[0]]
    for n, step in enumerate(STEPS[1:]):
        got.append(shift(blocks[n + 1], "z", NZ, step))
    part_a = jnp.concatenate(got[: NZ // 2])
    part_b = jnp.concatenate(got[NZ // 2 :])
    right_a = shift(part_a, "x", NX, 1)
    left_a = shift(part_a, "x", NX, -1)
    left_b = shift(part_b, "x", NX, -1)
    right_b = shift(part_b, "x", NX, 1)
    far_a = shift(right_a, "x", NX, 1)
    far_b = shift(left_b, "x", NX, -1)

    cot_own = lax.dynamic_slice_in_dim(cotangent, group * per, per, 0)
    cot_own = cot_own.reshape(per, NX, chunk).transpose(1, 0, 2)
    cot_send = jnp.broadcast_to(cot_own[None], (NZ, NX, per, chunk)).reshape(NZ * NX, per, chunk)
    cot0 = lax.all_to_all(cot_send, ("z", "x"), 0, 0, tiled=True)
    cot3 = shift(cot0, "y", NY, 1)
    cot1 = shift(cot0, "y", NY, -1)
    cot2 = shift(cot0, "y", NY, 2)
    cots = []
    for a in (cot0, cot1, cot2, cot3):
        b = shift(a, "c", NC, 1)
        cots += [a.reshape(NZ, NX, per, chunk), b.reshape(NZ, NX, per, chunk)]

    down_recv = lax.all_to_all(down, ("z", "x"), 0, 0, tiled=True)
    down_recv = down_recv.reshape(NZ, NX, PIECE, width)

    (main,) = hidden(COLS, (part_a, part_b, left_a, left_b, right_a, right_b), gate, up)
    main1 = shift(main, "x", NX, -1)
    late, full = hidden(NX, (far_a, far_b), gate, up, main)
    late1 = shift(late, "x", NX, -1)
    full3 = shift(full, "x", NX, -3)
    full2 = shift(full, "x", NX, -2)
    parts = {0: (full,), 1: (main1, late1), 2: (full2,), 3: (full3,)}
    near = (part_a, part_b, left_a, left_b, right_a, right_b)
    grad_near = pick(here, ORDER[:3], near, cots, width)
    grad_far = pick(here, ORDER[3:], (far_a, far_b), cots, width)

    slot_table = slot_lookup(cluster, merged_slot)
    expert_ids = jnp.arange(EXPERTS, dtype=jnp.int32)
    member = first_expert + jnp.arange(NZ, dtype=jnp.int32)
    member_slot = jnp.sum(
        jnp.where(member[:, None] == expert_ids[None, :], slot_table[None, :], 0), axis=1
    )
    owner, row = member_slot // OWN, member_slot % OWN
    core, hop = (owner % NC - c) % NC, (owner // NC - y) % NY
    spots = (core * NY + hop) * OWN + row

    groups = []
    for half in HALVES:
        denom = fisher_half(half, parts, grad_near, grad_far)
        denom_recv = lax.all_to_all(denom, ("z", "x"), 0, 0, tiled=True)
        mixed = mix(half, spots, denom_recv, down_recv)
        own2, snd2, own, snd = mixed
        groups.append(reduce_slots(snd2, snd, own2, own))
    first = ratio(groups[0])
    return final(first, groups[1])


def solution(mesh):
    fine = Mesh(mesh.devices.reshape(NY, NC, NZ, NX), ("y", "c", "z", "x"))
    rows = P(("z", "x"), None)
    units = P(("y", "c", "z", "x"), None)

    return jax.shard_map(
        per_device,
        mesh=fine,
        in_specs=(rows, rows, rows, rows, units, units, units, P(), P()),
        out_specs=P(("y", "c"), None, ("z", "x"), None),
        check_vma=False,
    )
```

```python
import functools

import jax
import jax.numpy as jnp
from jax import lax
from jax.experimental import pallas as pl
from jax.experimental.pallas import tpu as pltpu
from jax.sharding import Mesh, PartitionSpec as P


F = 1024
EXPERTS = 64
MERGED = 24
CAP = 20
PRIOR = 0.1
NY, NC, NZ, NX = 4, 2, 8, 4
OWN = MERGED // (NY * NC)
ROWS = NZ * CAP
TALL = 24
STEPS = (0, 1, 7, 2, 6, 3, 5, 4)
PIECE = F // (NZ * NX * NX)
HALVES = ((0, 1), (3, 2))
ORDER = (0, 1, 3, 2)
HOPS = (1, 3, 0)
COLS = 7
INTERPRET = False


bf16 = jnp.bfloat16
f32 = jnp.float32


def shift(a, axis, size, step):
    return lax.ppermute(a, axis, [(i, (i + step) % size) for i in range(size)])


def slot_lookup(cluster, merged_slot):
    ids = jnp.arange(MERGED, dtype=jnp.int32)
    return jnp.sum(jnp.where(cluster[:, None] == ids[None, :], merged_slot[None, :], 0), axis=1)


def pack_kernel(here_ref, route_ref, weight_ref, tok_ref, *refs):
    outs, pick_ref, scale_ref = refs[:NZ], refs[NZ], refs[NZ + 1]
    toks, width = tok_ref.shape
    per = toks // (NY * NC)
    y, c, z = here_ref[0], here_ref[1], here_ref[2]
    first = (y * NC + c) * NZ
    routes = route_ref[...]
    weights = weight_ref[...]
    marks, scales = [], []
    for step in STEPS:
        match = routes == first + lax.rem(z + step, NZ)
        marks.append(jnp.sum(jnp.where(match, 1.0, 0.0), axis=0, keepdims=True))
        scales.append(jnp.sum(jnp.where(match, weights, 0.0), axis=0, keepdims=True))
    row = lax.broadcasted_iota(jnp.int32, (toks, toks), 0)
    col = lax.broadcasted_iota(jnp.int32, (toks, toks), 1)
    before = jnp.where(row < col, 1.0, 0.0).astype(bf16)
    marked = jnp.concatenate(marks, axis=0)
    places = jnp.dot(marked.astype(bf16), before, preferred_element_type=f32)
    place = lax.broadcasted_iota(jnp.int32, (TALL, toks), 0).astype(f32)
    for n in range(NZ):
        hit = (places[n : n + 1] == place) & (marks[n] > 0.0)
        pick_ref[n * TALL : (n + 1) * TALL, :] = jnp.where(hit, 1.0, 0.0)
        scale_ref[n * TALL : (n + 1) * TALL, :] = jnp.where(hit, scales[n], 0.0)
    pick = pick_ref[...].astype(bf16)
    step = width // COLS

    def body(k, carry):
        cols = pl.ds(pl.multiple_of(k * step, step), step)
        rows = jnp.dot(pick, tok_ref[:, cols], preferred_element_type=f32).astype(bf16)
        for n, out in enumerate(outs):
            out[:, cols] = rows[n * TALL : n * TALL + CAP]
        return carry

    lax.fori_loop(0, COLS, body, 0)
    ahead = lax.rem(y + col // (NC * per), NY)
    other = lax.rem(c + lax.rem(col // per, NC), NC)
    turned = (ahead * NC + other) * per + lax.rem(col, per)
    turn = jnp.where(row == turned, 1.0, 0.0).astype(bf16)
    scale = scale_ref[...]
    high = scale.astype(bf16)
    low = (scale - high.astype(f32)).astype(bf16)
    high = jnp.dot(high, turn, preferred_element_type=f32)
    low = jnp.dot(low, turn, preferred_element_type=f32)
    tail = jnp.concatenate([high, low], axis=1).astype(bf16)
    for n, out in enumerate(outs):
        out[:, width:] = tail[n * TALL : n * TALL + CAP]


def pack(here, routes, weights, tokens):
    toks, width = tokens.shape
    shape = jax.ShapeDtypeStruct((CAP, width + 2 * toks), bf16)
    return pl.pallas_call(
        pack_kernel,
        in_specs=[pl.BlockSpec(memory_space=pltpu.SMEM)] + [pl.BlockSpec(memory_space=pltpu.VMEM)] * 3,
        out_shape=[shape] * NZ,
        scratch_shapes=[pltpu.VMEM((NZ * TALL, toks), f32)] * 2,
        interpret=INTERPRET,
        name="pack",
    )(here, routes.T, weights.T, tokens)


def pick_kernel(here_ref, *refs, ahead):
    count = 2 * len(ahead)
    tails, cots, out_ref, tail_ref = refs[:count], refs[count:-2], refs[-2], refs[-1]
    group = NZ // 2
    height = group * CAP
    per = cots[0].shape[2]
    tok = per * len(cots)
    row = lax.broadcasted_iota(jnp.int32, (height, group * tok), 0) // CAP
    col = lax.broadcasted_iota(jnp.int32, (height, group * tok), 1) // tok
    same = row == col
    lanes = tail_ref.shape[-1]
    lane = lax.broadcasted_iota(jnp.int32, (lanes, 2 * group * tok), 0)
    wide = lax.broadcasted_iota(jnp.int32, (lanes, 2 * group * tok), 1)
    match = (lane % tok == wide % tok) & (lane // tok == wide // (group * tok))
    spread = jnp.where(match, 1.0, 0.0).astype(bf16)
    z, x = here_ref[2], here_ref[3]
    for n, t in enumerate(tails):
        tail_ref[n] = t[...]

    def body(n, carry):
        half = n % 2
        turn = ahead[0]
        for i in range(1, len(ahead)):
            turn = jnp.where(n // 2 == i, ahead[i], turn)
        xs = lax.rem(x + turn, NX)
        wide = jnp.dot(tail_ref[n], spread, preferred_element_type=f32)
        high = jnp.where(same, wide[:, : group * tok], 0.0).astype(bf16)
        low = jnp.where(same, wide[:, group * tok :], 0.0).astype(bf16)
        blocks = []
        for j in range(group):
            step = jnp.where(half == 0, STEPS[j], STEPS[group + j])
            zs = lax.rem(z + NZ - step, NZ)
            blocks += [cot[zs, xs if cot.shape[1] > 1 else 0].astype(f32) for cot in cots]
        cot = jnp.concatenate(blocks, axis=0).astype(bf16)
        val = jnp.dot(high, cot, preferred_element_type=f32)
        val = val + jnp.dot(low, cot, preferred_element_type=f32)
        val = val.astype(bf16).astype(f32)
        out_ref[n] = (val * val).astype(bf16)
        return carry

    lax.fori_loop(0, count, body, 0)


def pick(here, ahead, pieces, cots, width):
    lanes = pieces[0].shape[1] - width
    height = pieces[0].shape[0]
    chunk = cots[0].shape[-1]
    count = len(pieces)
    tail = pl.BlockSpec((height, lanes), lambda i, src: (0, width // lanes))
    if len(ahead) > 1:
        part = lambda a: pl.BlockSpec(a.shape, lambda i, src: (0, 0, 0, 0))
    else:
        part = lambda a: pl.BlockSpec(
            (NZ, 1) + a.shape[2:], lambda i, src: (0, lax.rem(src[3] + ahead[0], NX), 0, 0)
        )
    return pl.pallas_call(
        functools.partial(pick_kernel, ahead=ahead),
        grid_spec=pltpu.PrefetchScalarGridSpec(
            num_scalar_prefetch=1,
            grid=(1,),
            in_specs=[tail] * count + [part(c) for c in cots],
            out_specs=pl.BlockSpec((count, ROWS // 2, chunk), lambda i, src: (0, 0, 0)),
            scratch_shapes=[pltpu.VMEM((count, height, lanes), bf16)],
        ),
        out_shape=jax.ShapeDtypeStruct((count, ROWS // 2, chunk), bf16),
        interpret=INTERPRET,
        name="pick",
    )(here, *pieces, *cots).reshape(count // 2, ROWS, chunk)


def hidden_kernel(*refs, pieces, known):
    blocks, gate_ref, up_ref = refs[:pieces], refs[pieces], refs[pieces + 1]
    outs, acc_ref = refs[pieces + 2 + known : -1], refs[-1]
    step = pl.program_id(0)
    rows = jnp.concatenate([b[...] for b in blocks], axis=0)
    units = gate_ref.shape[0]
    dims = (((1,), (1,)), ((), ()))
    g = lax.dot_general(rows, gate_ref[...], dims, preferred_element_type=f32)
    u = lax.dot_general(rows, up_ref[...], dims, preferred_element_type=f32)

    @pl.when(step == 0)
    def _():
        acc_ref[:, :units] = g
        acc_ref[:, units:] = u

    @pl.when(step > 0)
    def _():
        acc_ref[:, :units] += g
        acc_ref[:, units:] += u

    @pl.when(step == pl.num_programs(0) - 1)
    def _():
        gv = acc_ref[:, :units]
        h = gv / (1.0 + jnp.exp(-gv)) * acc_ref[:, units:]
        h = (h * h).astype(bf16)
        outs[0][...] = h
        if known:
            old = refs[pieces + 2]
            outs[1][: old.shape[0], :] = old[...]
            outs[1][old.shape[0] :, :] = h


def hidden(count, pieces, gate, up, *known):
    units, width = gate.shape
    step = width // count
    total = sum(p.shape[0] for p in pieces)
    col = lambda k: (0, k)
    fixed = lambda k: (0, 0)
    heights = [total] + [total + k.shape[0] for k in known]
    return pl.pallas_call(
        functools.partial(hidden_kernel, pieces=len(pieces), known=len(known)),
        grid=(count,),
        in_specs=[pl.BlockSpec((p.shape[0], step), col) for p in pieces]
        + [pl.BlockSpec((units, step), col)] * 2
        + [pl.BlockSpec(k.shape, fixed) for k in known],
        out_specs=[pl.BlockSpec((h, units), fixed) for h in heights],
        out_shape=[jax.ShapeDtypeStruct((h, units), bf16) for h in heights],
        scratch_shapes=[pltpu.VMEM((total, 2 * units), f32)],
        interpret=INTERPRET,
        name="hidden",
    )(*pieces, gate, up, *known)


def fisher_kernel(*refs, half, counts):
    near_ref, far_ref, out_ref = refs[-3:]
    grads = {r: near_ref.at[i] for i, r in enumerate(ORDER[:3])}
    grads[ORDER[3]] = far_ref.at[0]
    start = 0
    for j, count in enumerate(counts):
        e = half[j]
        parts = [r[...] for r in refs[start : start + count]]
        start += count
        h = jnp.concatenate(parts, axis=0) if count > 1 else parts[0]
        g = jnp.concatenate([grads[(e + d) % NX][...] for d in ORDER], axis=0)
        acc = lax.dot_general(h, g, (((0,), (0,)), ((), ())), preferred_element_type=f32)
        acc = acc + PRIOR
        out_ref[:, j * PIECE : (j + 1) * PIECE, :] = acc.reshape(-1, PIECE, acc.shape[1]).astype(bf16)


def fisher_half(half, parts, near, far):
    flat = [h for e in half for h in parts[e]]
    units = flat[0].shape[1] // 2
    chunk = near.shape[-1]
    return pl.pallas_call(
        functools.partial(fisher_kernel, half=half, counts=[len(parts[e]) for e in half]),
        grid=(2,),
        in_specs=[pl.BlockSpec((h.shape[0], units), lambda k: (0, k)) for h in flat]
        + [pl.BlockSpec(a.shape, lambda k: (0, 0, 0)) for a in (near, far)],
        out_specs=pl.BlockSpec((NZ * NX // 2, 2 * PIECE, chunk), lambda k: (k, 0, 0)),
        out_shape=jax.ShapeDtypeStruct((NZ * NX, 2 * PIECE, chunk), bf16),
        interpret=INTERPRET,
        name="fisher",
    )(*flat, near, far)


def mix_kernel(spot_ref, den_ref, da_ref, db_ref, *refs):
    two, rest, val_ref, acc_ref = refs[-6:-4], refs[-4:-2], refs[-2], refs[-1]
    den = den_ref[:, 0]
    down = jnp.concatenate([da_ref[:, 0].astype(f32), db_ref[:, 0].astype(f32)], axis=1)
    val_ref[0] = (den.astype(f32) * down).astype(bf16)
    val_ref[1] = den

    def body(arr, carry):
        acc_ref[...] = jnp.zeros(acc_ref.shape, bf16)
        for i in range(NZ):
            acc_ref[spot_ref[i]] += val_ref[arr, i]
        for core in range(NC):
            for hop in range(NY):
                start = (core * NY + hop) * OWN
                res = acc_ref[start : start + OWN]
                res = res.reshape(OWN * 2 * PIECE, res.shape[-1])
                if hop == 2:
                    two[core][arr] = res
                else:
                    rest[core][arr, HOPS.index(hop)] = res
        return carry

    lax.fori_loop(0, 2, body, 0)


def mix(half, spots, den, down):
    chunk = den.shape[-1]
    width = down.shape[-1]
    tall = 2 * OWN * PIECE
    two = jax.ShapeDtypeStruct((2, tall, width), bf16)
    rest = jax.ShapeDtypeStruct((2, len(HOPS), tall, width), bf16)
    two_spec = pl.BlockSpec((2, tall, chunk), lambda k: (0, 0, k))
    rest_spec = pl.BlockSpec((2, len(HOPS), tall, chunk), lambda k: (0, 0, 0, k))

    def down_spec(e):
        return pl.BlockSpec((NZ, 1, PIECE, chunk), lambda k: (0, lax.rem(k + e, NX), 0, k))

    return pl.pallas_call(
        mix_kernel,
        grid=(NX,),
        in_specs=[
            pl.BlockSpec(memory_space=pltpu.SMEM),
            pl.BlockSpec((NZ, 1, 2 * PIECE, chunk), lambda k: (0, k, 0, 0)),
            down_spec(half[0]),
            down_spec(half[1]),
        ],
        out_specs=[two_spec, two_spec, rest_spec, rest_spec],
        out_shape=[two, two, rest, rest],
        scratch_shapes=[
            pltpu.VMEM((2, NZ, 2 * PIECE, chunk), bf16),
            pltpu.VMEM((MERGED, 2 * PIECE, chunk), bf16),
        ],
        interpret=INTERPRET,
        name="mix",
    )(spots, den.reshape(NZ, NX, 2 * PIECE, chunk), down, down)


def ratio(group):
    own, oth, up_num, up_den, dn_num, dn_den = group
    num = [(own, (0, 2)), (oth, (0, 2)), (up_num, ()), (dn_num, ())]
    den = [(own, (1, 2)), (oth, (1, 2)), (up_den, ()), (dn_den, ())]
    return looped((num, den), True)[0]


def final_kernel(first_ref, own, oth, up_num, up_den, dn_num, dn_den, out_ref):
    k = pl.program_id(0)
    tot = []
    for arr, up, dn in ((0, up_num, dn_num), (1, up_den, dn_den)):
        tot.append(
            own[arr, 0].astype(f32) + oth[arr, 0].astype(f32) + up[...].astype(f32) + dn[...].astype(f32)
        )
    second = (tot[0] / tot[1]).astype(bf16)
    for half, res in zip(HALVES, (first_ref[...], second)):
        for j, e in enumerate(half):
            s = lax.rem(k + e, NX)
            for m in range(OWN):
                start = (2 * m + j) * PIECE
                out_ref[m, s] = res[start : start + PIECE]


def final(first, group):
    tall, width = first.shape
    chunk = width // NX
    flat = pl.BlockSpec((tall, chunk), lambda k: (0, k))
    rest = pl.BlockSpec((2, 1, tall, chunk), lambda k: (0, 2, 0, k))
    return pl.pallas_call(
        final_kernel,
        grid=(NX,),
        in_specs=[flat, rest, rest, flat, flat, flat, flat],
        out_specs=pl.BlockSpec((OWN, NX, PIECE, chunk), lambda k: (0, 0, 0, k)),
        out_shape=jax.ShapeDtypeStruct((OWN, NX, PIECE, width), bf16),
        interpret=INTERPRET,
        name="final",
    )(first, *group)


def looped_kernel(*refs, counts, divide):
    outs = refs[sum(counts) :]
    step = outs[0].shape[1] // COLS

    def body(k, carry):
        cols = pl.ds(pl.multiple_of(k * step, step), step)
        start = 0
        totals = []
        for count in counts:
            total = refs[start][:, cols].astype(f32)
            for r in refs[start + 1 : start + count]:
                total = total + r[:, cols].astype(f32)
            totals.append(total)
            start += count
        if divide:
            totals = [totals[0] / totals[1]]
        for out, total in zip(outs, totals):
            out[:, cols] = total.astype(bf16)
        return carry

    lax.fori_loop(0, COLS, body, 0)


def looped(groups, divide=False):
    specs, args = [], []
    for group in groups:
        for arr, lead in group:
            shape = (None,) * len(lead) + arr.shape[len(lead) :]
            specs.append(pl.BlockSpec(shape, lambda i, lead=lead: lead + (0, 0)))
            args.append(arr)
    shape = groups[0][0][0].shape[-2:]
    count = 1 if divide else len(groups)
    return pl.pallas_call(
        functools.partial(looped_kernel, counts=[len(g) for g in groups], divide=divide),
        grid=(1,),
        in_specs=specs,
        out_specs=[pl.BlockSpec(shape, lambda i: (0, 0))] * count,
        out_shape=[jax.ShapeDtypeStruct(shape, bf16)] * count,
        interpret=INTERPRET,
        name="looped",
    )(*args)


def sums(*groups):
    outs = []
    for group in groups:
        total = 0.0
        for arr, lead in group:
            total = total + arr[lead].astype(f32)
        outs.append(total.astype(bf16))
    return outs


def reduce_slots(n, snd2, snd, own2, own):
    oth2 = shift(snd2, "c", NC, 1)
    oth = shift(snd, "c", NC, 1)
    add = sums if n else lambda *groups: looped(groups)
    two_num, two_den = add([(own2, (0,)), (oth2, (0,))], [(own2, (1,)), (oth2, (1,))])
    one_den, three_num = add([(own, (1, 0)), (oth, (1, 0))], [(own, (0, 1)), (oth, (0, 1))])
    up1 = shift(two_num, "y", NY, 1)
    dn1 = shift(two_den, "y", NY, -1)
    up_den = shift(one_den, "y", NY, 1)
    dn_num = shift(three_num, "y", NY, -1)
    one_num, three_den = add(
        [(own, (0, 0)), (oth, (0, 0)), (up1, ())], [(own, (1, 1)), (oth, (1, 1)), (dn1, ())]
    )
    up_num = shift(one_num, "y", NY, 1)
    dn_den = shift(three_den, "y", NY, -1)
    return own, oth, up_num, up_den, dn_num, dn_den


def per_device(tokens, cotangent, routes, route_weights, gate, up, down, cluster, merged_slot):
    width = gate.shape[1]
    chunk = width // NX
    toks = tokens.shape[0]
    per = toks // (NY * NC)
    y, c = lax.axis_index("y"), lax.axis_index("c")
    z, x = lax.axis_index("z"), lax.axis_index("x")
    group = y * NC + c
    first_expert = group * NZ
    here = jnp.stack([y, c, z, x]).astype(jnp.int32)
    blocks = pack(here, routes, route_weights, tokens)
    got = [blocks[0]]
    for n, step in enumerate(STEPS[1:]):
        got.append(shift(blocks[n + 1], "z", NZ, step))
    part_a = jnp.concatenate(got[: NZ // 2])
    part_b = jnp.concatenate(got[NZ // 2 :])
    right_a = shift(part_a, "x", NX, 1)
    left_a = shift(part_a, "x", NX, -1)
    left_b = shift(part_b, "x", NX, -1)
    right_b = shift(part_b, "x", NX, 1)
    far_a = shift(right_a, "x", NX, 1)
    far_b = shift(left_b, "x", NX, -1)

    cot_own = lax.dynamic_slice_in_dim(cotangent, group * per, per, 0)
    cot_own = cot_own.reshape(per, NX, chunk).transpose(1, 0, 2)
    cot_send = jnp.broadcast_to(cot_own[None], (NZ, NX, per, chunk)).reshape(NZ * NX, per, chunk)
    cot0 = lax.all_to_all(cot_send, ("z", "x"), 0, 0, tiled=True)
    cot3 = shift(cot0, "y", NY, 1)
    cot1 = shift(cot0, "y", NY, -1)
    cot2 = shift(cot0, "y", NY, 2)
    cots = []
    for a in (cot0, cot1, cot2, cot3):
        b = shift(a, "c", NC, 1)
        cots += [a.reshape(NZ, NX, per, chunk), b.reshape(NZ, NX, per, chunk)]

    down_recv = lax.all_to_all(down, ("z", "x"), 0, 0, tiled=True)
    down_recv = down_recv.reshape(NZ, NX, PIECE, width)

    (main,) = hidden(2 * COLS, (part_a, part_b, left_a, left_b, right_a, right_b), gate, up)
    main1 = shift(main, "x", NX, -1)
    late, full = hidden(NX, (far_a, far_b), gate, up, main)
    late1 = shift(late, "x", NX, -1)
    full3 = shift(full, "x", NX, -3)
    full2 = shift(full, "x", NX, -2)
    parts = {0: (full,), 1: (main1, late1), 2: (full2,), 3: (full3,)}
    near = (part_a, part_b, left_a, left_b, right_a, right_b)
    grad_near = pick(here, ORDER[:3], near, cots, width)
    grad_far = pick(here, ORDER[3:], (far_a, far_b), cots, width)

    slot_table = slot_lookup(cluster, merged_slot)
    expert_ids = jnp.arange(EXPERTS, dtype=jnp.int32)
    member = first_expert + jnp.arange(NZ, dtype=jnp.int32)
    member_slot = jnp.sum(
        jnp.where(member[:, None] == expert_ids[None, :], slot_table[None, :], 0), axis=1
    )
    owner, row = member_slot // OWN, member_slot % OWN
    core, hop = (owner % NC - c) % NC, (owner // NC - y) % NY
    spots = (core * NY + hop) * OWN + row

    groups = []
    for n, half in enumerate(HALVES):
        denom = fisher_half(half, parts, grad_near, grad_far)
        denom_recv = lax.all_to_all(denom, ("z", "x"), 0, 0, tiled=True)
        mixed = mix(half, spots, denom_recv, down_recv)
        own2, snd2, own, snd = mixed
        groups.append(reduce_slots(n, snd2, snd, own2, own))
    first = ratio(groups[0])
    return final(first, groups[1])


def solution(mesh):
    fine = Mesh(mesh.devices.reshape(NY, NC, NZ, NX), ("y", "c", "z", "x"))
    rows = P(("z", "x"), None)
    units = P(("y", "c", "z", "x"), None)

    return jax.shard_map(
        per_device,
        mesh=fine,
        in_specs=(rows, rows, rows, rows, units, units, units, P(), P()),
        out_specs=P(("y", "c"), None, ("z", "x"), None),
        check_vma=False,
    )
```

```python
import functools

import jax
import jax.numpy as jnp
from jax import lax
from jax.experimental import pallas as pl
from jax.experimental.pallas import tpu as pltpu
from jax.sharding import Mesh, PartitionSpec as P


F = 1024
EXPERTS = 64
MERGED = 24
CAP = 20
PRIOR = 0.1
NY, NC, NZ, NX = 4, 2, 8, 4
OWN = MERGED // (NY * NC)
ROWS = NZ * CAP
TALL = 24
STEPS = (0, 1, 7, 2, 6, 3, 5, 4)
PIECE = F // (NZ * NX * NX)
HALVES = ((0, 1), (3, 2))
ORDER = (0, 1, 3, 2)
HOPS = (1, 3, 0)
COLS = 7
INTERPRET = False


bf16 = jnp.bfloat16
f32 = jnp.float32


def shift(a, axis, size, step):
    return lax.ppermute(a, axis, [(i, (i + step) % size) for i in range(size)])


def slot_lookup(cluster, merged_slot):
    ids = jnp.arange(MERGED, dtype=jnp.int32)
    return jnp.sum(jnp.where(cluster[:, None] == ids[None, :], merged_slot[None, :], 0), axis=1)


def pack_kernel(here_ref, route_ref, weight_ref, tok_ref, *refs):
    outs, pick_ref, scale_ref = refs[:NZ], refs[NZ], refs[NZ + 1]
    toks, width = tok_ref.shape
    per = toks // (NY * NC)
    y, c, z = here_ref[0], here_ref[1], here_ref[2]
    first = (y * NC + c) * NZ
    routes = route_ref[...]
    weights = weight_ref[...]
    marks, scales = [], []
    for step in STEPS:
        match = routes == first + lax.rem(z + step, NZ)
        marks.append(jnp.sum(jnp.where(match, 1.0, 0.0), axis=0, keepdims=True))
        scales.append(jnp.sum(jnp.where(match, weights, 0.0), axis=0, keepdims=True))
    row = lax.broadcasted_iota(jnp.int32, (toks, toks), 0)
    col = lax.broadcasted_iota(jnp.int32, (toks, toks), 1)
    before = jnp.where(row < col, 1.0, 0.0).astype(bf16)
    marked = jnp.concatenate(marks, axis=0)
    places = jnp.dot(marked.astype(bf16), before, preferred_element_type=f32)
    place = lax.broadcasted_iota(jnp.int32, (TALL, toks), 0).astype(f32)
    for n in range(NZ):
        hit = (places[n : n + 1] == place) & (marks[n] > 0.0)
        pick_ref[n * TALL : (n + 1) * TALL, :] = jnp.where(hit, 1.0, 0.0)
        scale_ref[n * TALL : (n + 1) * TALL, :] = jnp.where(hit, scales[n], 0.0)
    pick = pick_ref[...].astype(bf16)
    step = width // COLS

    def body(k, carry):
        cols = pl.ds(pl.multiple_of(k * step, step), step)
        rows = jnp.dot(pick, tok_ref[:, cols], preferred_element_type=f32).astype(bf16)
        for n, out in enumerate(outs):
            out[:, cols] = rows[n * TALL : n * TALL + CAP]
        return carry

    lax.fori_loop(0, COLS, body, 0)
    ahead = lax.rem(y + col // (NC * per), NY)
    other = lax.rem(c + lax.rem(col // per, NC), NC)
    turned = (ahead * NC + other) * per + lax.rem(col, per)
    turn = jnp.where(row == turned, 1.0, 0.0).astype(bf16)
    scale = scale_ref[...]
    high = scale.astype(bf16)
    low = (scale - high.astype(f32)).astype(bf16)
    high = jnp.dot(high, turn, preferred_element_type=f32)
    low = jnp.dot(low, turn, preferred_element_type=f32)
    tail = jnp.concatenate([high, low], axis=1).astype(bf16)
    for n, out in enumerate(outs):
        out[:, width:] = tail[n * TALL : n * TALL + CAP]


def pack(here, routes, weights, tokens):
    toks, width = tokens.shape
    shape = jax.ShapeDtypeStruct((CAP, width + 2 * toks), bf16)
    return pl.pallas_call(
        pack_kernel,
        in_specs=[pl.BlockSpec(memory_space=pltpu.SMEM)] + [pl.BlockSpec(memory_space=pltpu.VMEM)] * 3,
        out_shape=[shape] * NZ,
        scratch_shapes=[pltpu.VMEM((NZ * TALL, toks), f32)] * 2,
        interpret=INTERPRET,
        name="pack",
    )(here, routes.T, weights.T, tokens)


def pick_kernel(here_ref, *refs, ahead):
    count = 2 * len(ahead)
    tails, cots, out_ref, tail_ref = refs[:count], refs[count:-2], refs[-2], refs[-1]
    group = NZ // 2
    height = group * CAP
    per = cots[0].shape[2]
    tok = per * len(cots)
    row = lax.broadcasted_iota(jnp.int32, (height, group * tok), 0) // CAP
    col = lax.broadcasted_iota(jnp.int32, (height, group * tok), 1) // tok
    same = row == col
    lanes = tail_ref.shape[-1]
    lane = lax.broadcasted_iota(jnp.int32, (lanes, 2 * group * tok), 0)
    wide = lax.broadcasted_iota(jnp.int32, (lanes, 2 * group * tok), 1)
    match = (lane % tok == wide % tok) & (lane // tok == wide // (group * tok))
    spread = jnp.where(match, 1.0, 0.0).astype(bf16)
    z, x = here_ref[2], here_ref[3]
    for n, t in enumerate(tails):
        tail_ref[n] = t[...]

    def body(n, carry):
        half = n % 2
        turn = ahead[0]
        for i in range(1, len(ahead)):
            turn = jnp.where(n // 2 == i, ahead[i], turn)
        xs = lax.rem(x + turn, NX)
        wide = jnp.dot(tail_ref[n], spread, preferred_element_type=f32)
        high = jnp.where(same, wide[:, : group * tok], 0.0).astype(bf16)
        low = jnp.where(same, wide[:, group * tok :], 0.0).astype(bf16)
        blocks = []
        for j in range(group):
            step = jnp.where(half == 0, STEPS[j], STEPS[group + j])
            zs = lax.rem(z + NZ - step, NZ)
            blocks += [cot[zs, xs if cot.shape[1] > 1 else 0].astype(f32) for cot in cots]
        cot = jnp.concatenate(blocks, axis=0).astype(bf16)
        val = jnp.dot(high, cot, preferred_element_type=f32)
        val = val + jnp.dot(low, cot, preferred_element_type=f32)
        val = val.astype(bf16).astype(f32)
        out_ref[n] = (val * val).astype(bf16)
        return carry

    lax.fori_loop(0, count, body, 0)


def pick(here, ahead, pieces, cots, width):
    lanes = pieces[0].shape[1] - width
    height = pieces[0].shape[0]
    chunk = cots[0].shape[-1]
    count = len(pieces)
    tail = pl.BlockSpec((height, lanes), lambda i, src: (0, width // lanes))
    if len(ahead) > 1:
        part = lambda a: pl.BlockSpec(a.shape, lambda i, src: (0, 0, 0, 0))
    else:
        part = lambda a: pl.BlockSpec(
            (NZ, 1) + a.shape[2:], lambda i, src: (0, lax.rem(src[3] + ahead[0], NX), 0, 0)
        )
    return pl.pallas_call(
        functools.partial(pick_kernel, ahead=ahead),
        grid_spec=pltpu.PrefetchScalarGridSpec(
            num_scalar_prefetch=1,
            grid=(1,),
            in_specs=[tail] * count + [part(c) for c in cots],
            out_specs=pl.BlockSpec((count, ROWS // 2, chunk), lambda i, src: (0, 0, 0)),
            scratch_shapes=[pltpu.VMEM((count, height, lanes), bf16)],
        ),
        out_shape=jax.ShapeDtypeStruct((count, ROWS // 2, chunk), bf16),
        interpret=INTERPRET,
        name="pick",
    )(here, *pieces, *cots).reshape(count // 2, ROWS, chunk)


def hidden_kernel(*refs, pieces, known):
    blocks, gate_ref, up_ref = refs[:pieces], refs[pieces], refs[pieces + 1]
    outs, acc_ref = refs[pieces + 2 + known : -1], refs[-1]
    step = pl.program_id(0)
    rows = jnp.concatenate([b[...] for b in blocks], axis=0)
    units = gate_ref.shape[0]
    dims = (((1,), (1,)), ((), ()))
    g = lax.dot_general(rows, gate_ref[...], dims, preferred_element_type=f32)
    u = lax.dot_general(rows, up_ref[...], dims, preferred_element_type=f32)

    @pl.when(step == 0)
    def _():
        acc_ref[:, :units] = g
        acc_ref[:, units:] = u

    @pl.when(step > 0)
    def _():
        acc_ref[:, :units] += g
        acc_ref[:, units:] += u

    @pl.when(step == pl.num_programs(0) - 1)
    def _():
        gv = acc_ref[:, :units]
        h = gv / (1.0 + jnp.exp(-gv)) * acc_ref[:, units:]
        h = (h * h).astype(bf16)
        outs[0][...] = h
        if known:
            old = refs[pieces + 2]
            outs[1][: old.shape[0], :] = old[...]
            outs[1][old.shape[0] :, :] = h


def hidden(count, pieces, gate, up, *known):
    units, width = gate.shape
    step = width // count
    total = sum(p.shape[0] for p in pieces)
    col = lambda k: (0, k)
    fixed = lambda k: (0, 0)
    heights = [total] + [total + k.shape[0] for k in known]
    return pl.pallas_call(
        functools.partial(hidden_kernel, pieces=len(pieces), known=len(known)),
        grid=(count,),
        in_specs=[pl.BlockSpec((p.shape[0], step), col) for p in pieces]
        + [pl.BlockSpec((units, step), col)] * 2
        + [pl.BlockSpec(k.shape, fixed) for k in known],
        out_specs=[pl.BlockSpec((h, units), fixed) for h in heights],
        out_shape=[jax.ShapeDtypeStruct((h, units), bf16) for h in heights],
        scratch_shapes=[pltpu.VMEM((total, 2 * units), f32)],
        interpret=INTERPRET,
        name="hidden",
    )(*pieces, gate, up, *known)


def fisher_kernel(*refs, half, counts):
    near_ref, far_ref, out_ref = refs[-3:]
    grads = {r: near_ref.at[i] for i, r in enumerate(ORDER[:3])}
    grads[ORDER[3]] = far_ref.at[0]
    start = 0
    for j, count in enumerate(counts):
        e = half[j]
        parts = [r[...] for r in refs[start : start + count]]
        start += count
        h = jnp.concatenate(parts, axis=0) if count > 1 else parts[0]
        g = jnp.concatenate([grads[(e + d) % NX][...] for d in ORDER], axis=0)
        acc = lax.dot_general(h, g, (((0,), (0,)), ((), ())), preferred_element_type=f32)
        acc = acc + PRIOR
        out_ref[:, j * PIECE : (j + 1) * PIECE, :] = acc.reshape(-1, PIECE, acc.shape[1]).astype(bf16)


def fisher_half(half, parts, near, far):
    flat = [h for e in half for h in parts[e]]
    units = flat[0].shape[1] // 2
    chunk = near.shape[-1]
    return pl.pallas_call(
        functools.partial(fisher_kernel, half=half, counts=[len(parts[e]) for e in half]),
        grid=(2,),
        in_specs=[pl.BlockSpec((h.shape[0], units), lambda k: (0, k)) for h in flat]
        + [pl.BlockSpec(a.shape, lambda k: (0, 0, 0)) for a in (near, far)],
        out_specs=pl.BlockSpec((NZ * NX // 2, 2 * PIECE, chunk), lambda k: (k, 0, 0)),
        out_shape=jax.ShapeDtypeStruct((NZ * NX, 2 * PIECE, chunk), bf16),
        interpret=INTERPRET,
        name="fisher",
    )(*flat, near, far)


def mix_kernel(spot_ref, den_ref, da_ref, db_ref, *refs):
    two, rest, val_ref, acc_ref = refs[-6:-4], refs[-4:-2], refs[-2], refs[-1]
    den = den_ref[:, 0]
    down = jnp.concatenate([da_ref[:, 0].astype(f32), db_ref[:, 0].astype(f32)], axis=1)
    val_ref[0] = (den.astype(f32) * down).astype(bf16)
    val_ref[1] = den

    def body(arr, carry):
        acc_ref[...] = jnp.zeros(acc_ref.shape, bf16)
        for i in range(NZ):
            acc_ref[spot_ref[i]] += val_ref[arr, i]
        for core in range(NC):
            for hop in range(NY):
                start = (core * NY + hop) * OWN
                res = acc_ref[start : start + OWN]
                res = res.reshape(OWN * 2 * PIECE, res.shape[-1])
                if hop == 2:
                    two[core][arr] = res
                else:
                    rest[core][arr, HOPS.index(hop)] = res
        return carry

    lax.fori_loop(0, 2, body, 0)


def mix(half, spots, den, down):
    chunk = den.shape[-1]
    width = down.shape[-1]
    tall = 2 * OWN * PIECE
    two = jax.ShapeDtypeStruct((2, tall, width), bf16)
    rest = jax.ShapeDtypeStruct((2, len(HOPS), tall, width), bf16)
    two_spec = pl.BlockSpec((2, tall, chunk), lambda k: (0, 0, k))
    rest_spec = pl.BlockSpec((2, len(HOPS), tall, chunk), lambda k: (0, 0, 0, k))

    def down_spec(e):
        return pl.BlockSpec((NZ, 1, PIECE, chunk), lambda k: (0, lax.rem(k + e, NX), 0, k))

    return pl.pallas_call(
        mix_kernel,
        grid=(NX,),
        in_specs=[
            pl.BlockSpec(memory_space=pltpu.SMEM),
            pl.BlockSpec((NZ, 1, 2 * PIECE, chunk), lambda k: (0, k, 0, 0)),
            down_spec(half[0]),
            down_spec(half[1]),
        ],
        out_specs=[two_spec, two_spec, rest_spec, rest_spec],
        out_shape=[two, two, rest, rest],
        scratch_shapes=[
            pltpu.VMEM((2, NZ, 2 * PIECE, chunk), bf16),
            pltpu.VMEM((MERGED, 2 * PIECE, chunk), bf16),
        ],
        interpret=INTERPRET,
        name="mix",
    )(spots, den.reshape(NZ, NX, 2 * PIECE, chunk), down, down)


def ratio(group):
    own, oth, up_num, up_den, dn_num, dn_den = group
    num = [(own, (0, 2)), (oth, (0, 2)), (up_num, ()), (dn_num, ())]
    den = [(own, (1, 2)), (oth, (1, 2)), (up_den, ()), (dn_den, ())]
    return looped((num, den), True)[0]


def final_kernel(first_ref, own, oth, up_num, up_den, dn_num, dn_den, out_ref):
    k = pl.program_id(0)
    tot = []
    for arr, up, dn in ((0, up_num, dn_num), (1, up_den, dn_den)):
        tot.append(
            own[arr, 0].astype(f32) + oth[arr, 0].astype(f32) + up[...].astype(f32) + dn[...].astype(f32)
        )
    second = (tot[0] / tot[1]).astype(bf16)
    for half, res in zip(HALVES, (first_ref[...], second)):
        for j, e in enumerate(half):
            s = lax.rem(k + e, NX)
            for m in range(OWN):
                start = (2 * m + j) * PIECE
                out_ref[m, s] = res[start : start + PIECE]


def final(first, group):
    tall, width = first.shape
    chunk = width // NX
    flat = pl.BlockSpec((tall, chunk), lambda k: (0, k))
    rest = pl.BlockSpec((2, 1, tall, chunk), lambda k: (0, 2, 0, k))
    return pl.pallas_call(
        final_kernel,
        grid=(NX,),
        in_specs=[flat, rest, rest, flat, flat, flat, flat],
        out_specs=pl.BlockSpec((OWN, NX, PIECE, chunk), lambda k: (0, 0, 0, k)),
        out_shape=jax.ShapeDtypeStruct((OWN, NX, PIECE, width), bf16),
        interpret=INTERPRET,
        name="final",
    )(first, *group)


def looped_kernel(*refs, counts, divide):
    outs = refs[sum(counts) :]
    step = outs[0].shape[1] // COLS

    def body(k, carry):
        cols = pl.ds(pl.multiple_of(k * step, step), step)
        start = 0
        totals = []
        for count in counts:
            total = refs[start][:, cols].astype(f32)
            for r in refs[start + 1 : start + count]:
                total = total + r[:, cols].astype(f32)
            totals.append(total)
            start += count
        if divide:
            totals = [totals[0] / totals[1]]
        for out, total in zip(outs, totals):
            out[:, cols] = total.astype(bf16)
        return carry

    lax.fori_loop(0, COLS, body, 0)


def looped(groups, divide=False):
    specs, args = [], []
    for group in groups:
        for arr, lead in group:
            shape = (None,) * len(lead) + arr.shape[len(lead) :]
            specs.append(pl.BlockSpec(shape, lambda i, lead=lead: lead + (0, 0)))
            args.append(arr)
    shape = groups[0][0][0].shape[-2:]
    count = 1 if divide else len(groups)
    return pl.pallas_call(
        functools.partial(looped_kernel, counts=[len(g) for g in groups], divide=divide),
        grid=(1,),
        in_specs=specs,
        out_specs=[pl.BlockSpec(shape, lambda i: (0, 0))] * count,
        out_shape=[jax.ShapeDtypeStruct(shape, bf16)] * count,
        interpret=INTERPRET,
        name="looped",
    )(*args)


def sums(*groups):
    outs = []
    for group in groups:
        total = 0.0
        for arr, lead in group:
            total = total + arr[lead].astype(f32)
        outs.append(total.astype(bf16))
    return outs


def reduce_slots(snd2, snd, own2, own):
    oth2 = shift(snd2, "c", NC, 1)
    oth = shift(snd, "c", NC, 1)
    two_num, two_den = sums([(own2, (0,)), (oth2, (0,))], [(own2, (1,)), (oth2, (1,))])
    one_den, three_num = sums([(own, (1, 0)), (oth, (1, 0))], [(own, (0, 1)), (oth, (0, 1))])
    up1 = shift(two_num, "y", NY, 1)
    dn1 = shift(two_den, "y", NY, -1)
    up_den = shift(one_den, "y", NY, 1)
    dn_num = shift(three_num, "y", NY, -1)
    one_num, three_den = sums(
        [(own, (0, 0)), (oth, (0, 0)), (up1, ())], [(own, (1, 1)), (oth, (1, 1)), (dn1, ())]
    )
    up_num = shift(one_num, "y", NY, 1)
    dn_den = shift(three_den, "y", NY, -1)
    return own, oth, up_num, up_den, dn_num, dn_den


def per_device(tokens, cotangent, routes, route_weights, gate, up, down, cluster, merged_slot):
    width = gate.shape[1]
    chunk = width // NX
    toks = tokens.shape[0]
    per = toks // (NY * NC)
    y, c = lax.axis_index("y"), lax.axis_index("c")
    z, x = lax.axis_index("z"), lax.axis_index("x")
    group = y * NC + c
    first_expert = group * NZ
    here = jnp.stack([y, c, z, x]).astype(jnp.int32)
    blocks = pack(here, routes, route_weights, tokens)
    got = [blocks[0]]
    for n, step in enumerate(STEPS[1:]):
        got.append(shift(blocks[n + 1], "z", NZ, step))
    part_a = jnp.concatenate(got[: NZ // 2])
    part_b = jnp.concatenate(got[NZ // 2 :])
    right_a = shift(part_a, "x", NX, 1)
    left_a = shift(part_a, "x", NX, -1)
    left_b = shift(part_b, "x", NX, -1)
    right_b = shift(part_b, "x", NX, 1)
    far_a = shift(right_a, "x", NX, 1)
    far_b = shift(left_b, "x", NX, -1)

    cot_own = lax.dynamic_slice_in_dim(cotangent, group * per, per, 0)
    cot_own = cot_own.reshape(per, NX, chunk).transpose(1, 0, 2)
    cot_send = jnp.broadcast_to(cot_own[None], (NZ, NX, per, chunk)).reshape(NZ * NX, per, chunk)
    cot0 = lax.all_to_all(cot_send, ("z", "x"), 0, 0, tiled=True)
    cot3 = shift(cot0, "y", NY, 1)
    cot1 = shift(cot0, "y", NY, -1)
    cot2 = shift(cot0, "y", NY, 2)
    cots = []
    for a in (cot0, cot1, cot2, cot3):
        b = shift(a, "c", NC, 1)
        cots += [a.reshape(NZ, NX, per, chunk), b.reshape(NZ, NX, per, chunk)]

    down_recv = lax.all_to_all(down, ("z", "x"), 0, 0, tiled=True)
    down_recv = down_recv.reshape(NZ, NX, PIECE, width)

    (main,) = hidden(COLS, (part_a, part_b, left_a, left_b, right_a, right_b), gate, up)
    main1 = shift(main, "x", NX, -1)
    late, full = hidden(NX, (far_a, far_b), gate, up, main)
    late1 = shift(late, "x", NX, -1)
    full3 = shift(full, "x", NX, -3)
    main2 = shift(main1, "x", NX, -1)
    late2 = shift(late1, "x", NX, -1)
    parts = {0: (full,), 1: (main1, late1), 2: (main2, late2), 3: (full3,)}
    near = (part_a, part_b, left_a, left_b, right_a, right_b)
    grad_near = pick(here, ORDER[:3], near, cots, width)
    grad_far = pick(here, ORDER[3:], (far_a, far_b), cots, width)

    slot_table = slot_lookup(cluster, merged_slot)
    expert_ids = jnp.arange(EXPERTS, dtype=jnp.int32)
    member = first_expert + jnp.arange(NZ, dtype=jnp.int32)
    member_slot = jnp.sum(
        jnp.where(member[:, None] == expert_ids[None, :], slot_table[None, :], 0), axis=1
    )
    owner, row = member_slot // OWN, member_slot % OWN
    core, hop = (owner % NC - c) % NC, (owner // NC - y) % NY
    spots = (core * NY + hop) * OWN + row

    groups = []
    for half in HALVES:
        denom = fisher_half(half, parts, grad_near, grad_far)
        denom_recv = lax.all_to_all(denom, ("z", "x"), 0, 0, tiled=True)
        mixed = mix(half, spots, denom_recv, down_recv)
        own2, snd2, own, snd = mixed
        groups.append(reduce_slots(snd2, snd, own2, own))
    first = ratio(groups[0])
    return final(first, groups[1])


def solution(mesh):
    fine = Mesh(mesh.devices.reshape(NY, NC, NZ, NX), ("y", "c", "z", "x"))
    rows = P(("z", "x"), None)
    units = P(("y", "c", "z", "x"), None)

    return jax.shard_map(
        per_device,
        mesh=fine,
        in_specs=(rows, rows, rows, rows, units, units, units, P(), P()),
        out_specs=P(("y", "c"), None, ("z", "x"), None),
        check_vma=False,
    )
```
